32 devices in a mesh: grp: 2 (over x), row: 16 (over z, y, core).
Axes of the slice: x: 2, y: 2, z: 4, core: 2. Of those that a mesh axis runs over, the one named last changes fastest.
Arguments:
- pair_map: bfloat16 [256, 128, 128], P(('grp', 'row')), parts along dimension 0, may hold values from -6 to 6
- norm_gain: float32 [128], replicated, may hold values from 0.1 to 1.9
- w_query: bfloat16 [128, 128], replicated, may hold values from -30 to 30
- w_key: bfloat16 [128, 128], replicated, may hold values from -1 to 1
- w_value: bfloat16 [128, 128], replicated, may hold values from -0.5 to 0.5
- w_gate: bfloat16 [128, 128], replicated, may hold values from -0.5 to 0.5
- w_bias: bfloat16 [128, 4], replicated, may hold values from -12 to 12
- w_output: bfloat16 [128, 128], replicated, may hold values from -0.5 to 0.5
- window_start: int32 [256], P(('grp', 'row')), parts along dimension 0, may hold values from 0 to 63
- key_length: int32 [256], P(('grp', 'row')), parts along dimension 0, may hold values from 32 to 64
Outputs:
- update: bfloat16 [256, 128, 128], P('grp', 'row'), parts along dimension 0
The draws below stay inside these ranges and needn't reach their ends.
There are 2 independent parts, one for each index of `grp`. The reference program is written for one: setup_inputs(seed, part) draws one part's arguments, and reference() takes and returns one part's arrays. A program takes and returns all parts, laid end to end along the dimension named above; an argument that names none is the same for every part. Nothing has to cross between parts.
All inputs are finite; a program needn't handle non-finite values.
Results may differ from the reference program's by a relative error of at most 0.0025.
The reference program's roundings to bfloat16 on the way (of `normed`, `weights` and `gated`) count: a program that leaves them out, or rounds other values in their place, can miss the bound.
Values may be sent and summed in bfloat16 or wider, within the bound.
A program may use at most 128 MiB of HBM per device.

```python
import jax
import jax.numpy as jnp
from jax import lax

C = 128
H = 4
DH = 32
N = 128


def paired_base(key):
    base = jax.random.fold_in(key, 4111)
    scale = C ** (-0.5)
    shared = jnp.clip(jax.random.normal(jax.random.fold_in(base, 1), (C, C), jnp.float32), -3.0, 3.0) * scale
    return (base, shared)


def draw_w_key(key, part):
    base, shared = paired_base(key)
    return shared.astype(jnp.bfloat16)


def draw_w_query(key, part):
    base, shared = paired_base(key)
    scale = C ** (-0.5)
    noise = jnp.clip(jax.random.normal(jax.random.fold_in(base, 2), (C, C), jnp.float32), -3.0, 3.0) * scale
    result = noise
    return jnp.clip(result, -30.0, 30.0).astype(jnp.bfloat16)


def draw_w_bias(key, part):
    base, shared = paired_base(key)
    scale = C ** (-0.5)
    raw = jnp.clip(jax.random.normal(jax.random.fold_in(base, 5), (C, H), jnp.float32), -3.0, 3.0) * scale
    result = raw * 1.5
    return jnp.clip(result, -12.0, 12.0).astype(jnp.bfloat16)


def place_ends(entries, own_key, least, top_value):
    longest = entries.shape.index(max(entries.shape))
    spots = []
    for shift in (0, 1):
        where = [jax.random.randint(jax.random.fold_in(own_key, axis), (), 0, length) for axis, length in enumerate(entries.shape)]
        where[longest] = (where[longest] + shift) % entries.shape[longest]
        spots.append(tuple(where))
    return entries.at[spots[0]].set(least).at[spots[1]].set(top_value)


def levels(stream_key, dims, pieces, smallest, high):
    factor_of, own = 1.0, jax.random.fold_in(stream_key, 6)
    for axis_at, parts in pieces:
        heights = jnp.exp(jax.random.uniform(jax.random.fold_in(own, axis_at), (parts,), jnp.float32, smallest / len(pieces), high / len(pieces)))
        factor_of = factor_of * jnp.repeat(heights, dims[axis_at] // parts).reshape([-1 if axis == axis_at else 1 for axis in range(len(dims))])
    return factor_of


def normal_values(stream_key, dims, scale, reach, split=(), kind=jnp.bfloat16):
    values = jax.random.normal(stream_key, dims, jnp.float32) * scale
    if len(split) > 0:
        values = levels(stream_key, dims, split, -0.22, 0.18) * values
    return jnp.clip(values, min=-reach, max=reach).astype(kind)


def setup_inputs(seed: int = 0, part: int = 0) -> dict:
    keys = jax.random.split(jax.random.key(seed), 11)
    part_keys = jax.random.split(jax.random.fold_in(keys[10], part), 11)
    return {
        "pair_map": normal_values(part_keys[0], (N, N, C), 1.0, 6.0, ((0, 16),)),
        "norm_gain": jnp.clip(1.0 + 0.18 * jax.random.normal(keys[1], (C,), jnp.float32), 0.1, 1.9),
        "w_query": draw_w_query(jax.random.fold_in(keys[10], 71), part),
        "w_key": draw_w_key(jax.random.fold_in(keys[10], 71), part),
        "w_value": normal_values(keys[4], (C, C), C ** -0.5, 0.5),
        "w_gate": normal_values(keys[5], (C, C), C ** -0.5, 0.5),
        "w_bias": draw_w_bias(jax.random.fold_in(keys[10], 71), part),
        "w_output": normal_values(keys[7], (C, C), C ** -0.5, 0.5),
        "window_start": place_ends(jax.random.randint(part_keys[8], (N,), 0, N // 2), jax.random.fold_in(part_keys[8], 1), 0, (N // 2) - 1).astype(jnp.int32),
        "key_length": place_ends(jax.random.randint(part_keys[9], (N,), N // 4, N // 2 + 1), jax.random.fold_in(part_keys[9], 1), N // 4, (N // 2 + 1) - 1).astype(jnp.int32),
    }


def normalize(rows, norm_gain):
    values = rows.astype(jnp.float32)
    center = lax.optimization_barrier(jnp.mean(values, axis=-1, keepdims=True))
    spread = lax.optimization_barrier(jnp.mean((values - center) ** 2, axis=-1, keepdims=True))
    return ((values - center) * lax.rsqrt(spread + 1e-05) * norm_gain).astype(jnp.bfloat16)

def reference(pair_map, norm_gain, w_query, w_key, w_value, w_gate, w_bias, w_output, window_start, key_length):
    positions = jnp.arange(N, dtype=jnp.int32)

    def bias_row(row_data):
        normed = normalize(row_data, norm_gain)
        return jnp.dot(normed, w_bias, preferred_element_type=jnp.float32)
    bias = lax.map(bias_row, pair_map)
    bias = jnp.transpose(bias, (2, 0, 1)).astype(jnp.float32)

    def one_row(inputs):
        row_data, first, count = inputs
        normed = normalize(row_data, norm_gain)
        query = jnp.dot(normed, w_query, preferred_element_type=jnp.float32).astype(jnp.bfloat16)
        key = jnp.dot(normed, w_key, preferred_element_type=jnp.float32).astype(jnp.bfloat16)
        value = jnp.dot(normed, w_value, preferred_element_type=jnp.float32).astype(jnp.bfloat16)
        gate = jnp.dot(normed, w_gate, preferred_element_type=jnp.float32).astype(jnp.bfloat16)
        query = query.astype(jnp.float32).reshape(N, H, DH)
        key = key.astype(jnp.float32).reshape(N, H, DH)
        value = value.astype(jnp.float32).reshape(N, H, DH)
        scores = jnp.einsum('jhd,khd->hjk', query, key) * (1.0 / DH ** 0.5) + bias
        valid = (positions >= first) & (positions < first + count)
        scores = jnp.where(valid[None, None, :], scores, jnp.float32(-1e+30))
        top = lax.optimization_barrier(jnp.max(scores, axis=-1, keepdims=True))
        raised = jnp.exp(scores - top)
        weights = (raised / lax.optimization_barrier(jnp.sum(raised, axis=-1, keepdims=True))).astype(jnp.bfloat16)
        attended = jnp.einsum('hjk,khd->jhd', weights.astype(jnp.float32), value).reshape(N, C)
        gated = (jax.nn.sigmoid(gate.astype(jnp.float32)) * attended).astype(jnp.bfloat16)
        return jnp.dot(gated, w_output, preferred_element_type=jnp.float32).astype(jnp.bfloat16)
    return lax.map(one_row, (pair_map, window_start, key_length))
```

```python
import functools
import math

import jax
import jax.numpy as jnp
from jax import lax
from jax.experimental import pallas as pl
from jax.experimental.pallas import tpu as pltpu
from jax.sharding import PartitionSpec as P

H = 4
LOG2E = math.log2(math.e)
MESH = pl.DeviceIdType.MESH
NT = (((1,), (1,)), ((), ()))
TN = (((0,), (0,)), ((), ()))
PIECES = 4


def other(index, step, count):
    if count & (count - 1):
        return lax.rem(index + step, count)
    result, bit = 0, 1
    while bit < count:
        a, b = index // bit % 2, step // bit % 2
        result = result + (a + b - 2 * a * b) * bit
        bit *= 2
    return result


def kernel(
    n,
    x_hbm,
    gain_hbm,
    wq_hbm,
    wk_hbm,
    wv_hbm,
    wg_hbm,
    wb_hbm,
    wo_hbm,
    start_hbm,
    length_hbm,
    out_ref,
    x_ref,
    gain_ref,
    asking_ref,
    giving_ref,
    wb_ref,
    wo_ref,
    bias_ref,
    turned_ref,
    score_ref,
    query_ref,
    key_ref,
    value_ref,
    sig_ref,
    send_ref,
    bound_ref,
    start_ref,
    length_ref,
    in_sem,
    bias_send,
    bias_recv,
    mate_send,
    mate_recv,
    out_send,
    out_recv,
):
    both, width, channels = x_ref.shape
    rows = both // 2
    head = channels // H
    chips = n // 2
    pairs = chips // 2
    couples = both // 2
    lanes = H * 4 * rows
    unrolled = chips <= 8
    me = lax.axis_index("row")
    core, chip = me % 2, me // 2
    pair = chip // 2
    mate = me + 1 - 2 * core
    steps = list(range(pairs // 2, pairs)) + list(range(0, pairs // 2))
    piece = max(1, rows // PIECES)

    def load(source, target, slot):
        copy = pltpu.make_async_copy(source, target, in_sem.at[slot])
        copy.start()
        return copy

    x_in = [
        load(x_hbm.at[pl.ds(at, piece)], x_ref.at[pl.ds(core * rows + at, piece)], 9 + at)
        for at in range(0, rows, piece)
    ]
    first_in = [load(gain_hbm, gain_ref, 0), load(wb_hbm, wb_ref, 1)]
    barrier = pltpu.get_barrier_semaphore()

    def greet(step, carry):
        peer = other(chip, step, chips) * 2 + core
        pl.semaphore_signal(barrier, inc=1, device_id={"row": peer}, device_id_type=MESH)
        return carry

    lax.fori_loop(1, chips, greet, 0, unroll=unrolled)
    pl.semaphore_signal(barrier, inc=1, device_id={"row": mate}, device_id_type=MESH)

    left, right = pl.ds(0, channels), pl.ds(channels, channels)
    window_in = [load(start_hbm, start_ref, 2), load(length_hbm, length_ref, 3)]
    weights_in = [
        load(source, target, 4 + at)
        for at, (source, target) in enumerate(
            (
                (wq_hbm, asking_ref.at[:, left]),
                (wg_hbm, asking_ref.at[:, right]),
                (wk_hbm, giving_ref.at[:, left]),
                (wv_hbm, giving_ref.at[:, right]),
                (wo_hbm, wo_ref),
            )
        )
    ]

    for copy in first_in:
        copy.wait()
    bias_weight = wb_ref[...]
    gain = gain_ref[...]
    ones = jnp.ones((channels, channels), jnp.bfloat16)
    for i in range(rows):
        if i % piece == 0:
            x_in[i // piece].wait()
        row = x_ref[core * rows + i]
        center = jnp.dot(row, ones, preferred_element_type=jnp.float32) * (1.0 / channels)
        values = row.astype(jnp.float32) - center
        spread = jnp.mean(values * values, axis=-1, keepdims=True)
        row = (values * lax.rsqrt(spread + 1e-05) * gain).astype(jnp.bfloat16)
        x_ref[core * rows + i] = row
        local = lax.dot_general(bias_weight, row, NT, preferred_element_type=jnp.float32)
        local = local * LOG2E
        for h in range(H):
            bias_ref[chip, h, i : i + 1, :] = local[h : h + 1]
    for copy in window_in:
        copy.wait()
    second = lax.broadcasted_iota(jnp.int32, (1, lanes), 1) // (2 * rows) % 2 == 1
    bounds = []
    for i in range(0, rows, 2):
        first = jnp.where(second, start_ref[i + 1], start_ref[i])
        count = jnp.where(second, length_ref[i + 1], length_ref[i])
        bounds += [first, first + count]
    own_bounds = pl.ds(pl.multiple_of(core * rows, rows), rows)
    bound_ref[own_bounds, :] = jnp.concatenate(bounds, axis=0).astype(jnp.float32)

    pl.semaphore_wait(barrier, chips)

    def bias_copy(source, target):
        return pltpu.make_async_remote_copy(
            src_ref=bias_ref.at[source],
            dst_ref=bias_ref.at[source],
            send_sem=bias_send,
            recv_sem=bias_recv.at[source],
            device_id={"row": target * 2 + core},
            device_id_type=MESH,
        )

    def mate_copy(ref, slot):
        return pltpu.make_async_remote_copy(
            src_ref=ref.at[own_bounds],
            dst_ref=ref.at[own_bounds],
            send_sem=mate_send.at[slot],
            recv_sem=mate_recv.at[slot],
            device_id={"row": mate},
            device_id_type=MESH,
        )

    def send_bias(step, carry):
        peer = other(pair, step, pairs) * 2
        bias_copy(chip, peer).start()
        bias_copy(chip, peer + 1).start()
        return carry

    neighbour = chip + 1 - 2 * (chip % 2)
    x_copy, bound_copy = mate_copy(x_ref, 0), mate_copy(bound_ref, 1)
    lax.fori_loop(pairs // 2, pairs, send_bias, 0, unroll=unrolled)
    x_copy.start()
    bound_copy.start()
    lax.fori_loop(1, pairs // 2, send_bias, 0, unroll=unrolled)
    bias_copy(chip, neighbour).start()

    for copy in weights_in:
        copy.wait()
    lane = lax.broadcasted_iota(jnp.int32, (1, channels), 1) // head
    masks = [(lane == h).astype(jnp.float32).astype(jnp.bfloat16) for h in range(H)]
    factor = LOG2E / head**0.5

    def project(i, couple, side):
        row = x_ref[i]
        parts = row.astype(jnp.float32).reshape(chips, 2, rows, channels)
        parts = jnp.where(core == 0, parts[:, 0], parts[:, 1])
        asking = parts.reshape(chips * rows, channels).astype(jnp.bfloat16)
        asked = jnp.dot(asking, asking_ref[...], preferred_element_type=jnp.float32)
        query_ref[i] = asked[:, :channels].astype(jnp.bfloat16)
        gate = asked[:, channels:].astype(jnp.bfloat16).astype(jnp.float32)
        sig_ref[i] = jax.nn.sigmoid(gate)
        given = jnp.dot(row, giving_ref[...], preferred_element_type=jnp.float32)
        given = given.astype(jnp.bfloat16)
        span = slice(side * channels, (side + 1) * channels)
        key_ref[couple, :, span] = given[:, :channels]
        value_ref[couple, :, span] = given[:, channels:]

    place = lax.broadcasted_iota(jnp.int32, (width, lanes), 0).astype(jnp.float32)
    wide = 2 * rows
    nothing = jnp.zeros((wide, channels), jnp.bfloat16)

    def score(couple):
        first = bound_ref[pl.ds(2 * couple, 1), :]
        last = bound_ref[pl.ds(2 * couple + 1, 1), :]
        valid = (place >= first) & (place < last)
        keys = key_ref[couple]
        for at in range(pairs):
            queries = [query_ref[2 * couple + side, at * wide : (at + 1) * wide, :] for side in range(2)]
            spread_out = []
            for h in range(H):
                spread_out.append(jnp.concatenate([queries[0] * masks[h], nothing], axis=1))
                spread_out.append(jnp.concatenate([nothing, queries[1] * masks[h]], axis=1))
            part = lax.dot_general(
                keys, jnp.concatenate(spread_out, axis=0), NT, preferred_element_type=jnp.float32
            )
            score_ref[at, couple] = jnp.where(valid, part * factor, jnp.float32(-1e30))

    def prepare(which):
        first = which * (rows // 2)
        if width <= 128:
            for at in range(rows):
                project(which * rows + at, first + at // 2, at % 2)
            for at in range(rows // 2):
                score(first + at)
        else:

            @pl.loop(0, rows // 2)
            def _(at):
                for side in range(2):
                    project(which * rows + 2 * at + side, first + at, side)
                score(first + at)

    prepare(core)
    x_copy.wait_recv()
    bound_copy.wait_recv()
    prepare(1 - core)

    def turn(peer):
        blocks = []
        for h in range(H):
            blocks += [bias_ref[peer * 2, h], bias_ref[peer * 2 + 1, h]] * 2
        turned_ref[...] = jnp.concatenate(blocks, axis=0).T

    def attend(peer, couple):
        t = score_ref[peer, couple] + turned_ref[...]
        raised = jnp.exp2(t - jnp.max(t, axis=0, keepdims=True))
        total = jnp.sum(raised, axis=0, keepdims=True)
        weights = (raised * (1.0 / total)).astype(jnp.bfloat16)
        mixed = lax.dot_general(
            weights, value_ref[couple], TN, preferred_element_type=jnp.float32
        )
        columns = pl.ds(pl.multiple_of(peer * wide, wide), wide)
        results = []
        for side in range(2):
            span = slice(side * channels, (side + 1) * channels)
            attended = mixed[side * wide : (side + 1) * wide, span]
            for h in range(1, H):
                at = (2 * h + side) * wide
                attended = jnp.where(lane == h, mixed[at : at + wide, span], attended)
            gated = sig_ref[2 * couple + side, columns, :] * attended
            results.append(gated.astype(jnp.bfloat16))
        return results

    def out_copy(target, part):
        return pltpu.make_async_remote_copy(
            src_ref=send_ref.at[target, pl.ds(part * rows, rows)],
            dst_ref=out_ref.at[pl.ds(pl.multiple_of(chip * both + part * rows, rows), rows)],
            send_sem=out_send,
            recv_sem=out_recv,
            device_id={"row": target * 2 + core},
            device_id_type=MESH,
        )

    def finish(peer, own):
        turn(peer)
        for part in range(2):
            gated = []
            for at in range(rows // 2):
                gated += attend(peer, part * (rows // 2) + at)
            update = jnp.dot(
                jnp.concatenate(gated, axis=0), wo_ref[...], preferred_element_type=jnp.float32
            ).reshape(rows, 2, rows, channels)
            for q in range(2):
                send_ref[peer * 2 + q, part * rows : (part + 1) * rows] = update[:, q].astype(
                    jnp.bfloat16
                )
            if own:
                out_copy(neighbour, part).start()
                here = pl.ds(pl.multiple_of(chip * both + part * rows, rows), rows)
                out_ref[here] = send_ref[chip, part * rows : (part + 1) * rows]
            else:
                for q in range(2):
                    out_copy(peer * 2 + q, part).start()

    def one_pair(step):
        peer = other(pair, step, pairs)
        for q in range(2):
            bias_copy(peer * 2 + q, chip).wait_recv()
        finish(peer, False)

    if unrolled:
        for step in range(max(pairs // 2, 1), pairs):
            one_pair(step)
        for step in range(1, pairs // 2):
            one_pair(step)
    else:
        pl.loop(pairs // 2, pairs)(one_pair)
        pl.loop(1, pairs // 2)(one_pair)
    bias_copy(neighbour, chip).wait_recv()
    finish(pair, True)

    x_copy.wait_send()
    bound_copy.wait_send()
    rest = pltpu.make_async_remote_copy(
        src_ref=bias_ref.at[pl.ds(0, chips - 1)],
        dst_ref=bias_ref.at[pl.ds(0, chips - 1)],
        send_sem=bias_send,
        recv_sem=bias_recv.at[chip],
        device_id={"row": mate},
        device_id_type=MESH,
    )
    rest.wait_send()
    rest = pltpu.make_async_remote_copy(
        src_ref=send_ref.at[pl.ds(0, chips - 1)],
        dst_ref=out_ref.at[pl.ds(0, (chips - 1) * both)],
        send_sem=out_send,
        recv_sem=out_recv,
        device_id={"row": mate},
        device_id_type=MESH,
    )
    rest.wait_send()
    rest.wait_recv()


def local(
    n, pair_map, norm_gain, w_query, w_key, w_value, w_gate, w_bias, w_output, window_start, key_length
):
    rows, width, channels = pair_map.shape
    chips = n // 2
    lanes = H * 4 * rows
    outside = pl.BlockSpec(memory_space=pltpu.HBM)
    return pl.pallas_call(
        functools.partial(kernel, n),
        out_shape=pltpu.VMEM((n * rows, width // n, channels), jnp.bfloat16),
        in_specs=[outside] * 10,
        out_specs=pl.BlockSpec(memory_space=pltpu.VMEM),
        scratch_shapes=[
            pltpu.VMEM((2 * rows, width, channels), jnp.bfloat16),
            pltpu.VMEM((1, channels), jnp.float32),
            pltpu.VMEM((channels, 2 * channels), jnp.bfloat16),
            pltpu.VMEM((channels, 2 * channels), jnp.bfloat16),
            pltpu.VMEM((H, channels), jnp.bfloat16),
            pltpu.VMEM((channels, channels), jnp.bfloat16),
            pltpu.VMEM((chips, H, rows, width), jnp.float32),
            pltpu.VMEM((width, lanes), jnp.float32),
            pltpu.VMEM((chips // 2, rows, width, lanes), jnp.float32),
            pltpu.VMEM((2 * rows, width // 2, channels), jnp.bfloat16),
            pltpu.VMEM((rows, width, 2 * channels), jnp.bfloat16),
            pltpu.VMEM((rows, width, 2 * channels), jnp.bfloat16),
            pltpu.VMEM((2 * rows, width // 2, channels), jnp.float32),
            pltpu.VMEM((chips, 2 * rows, width // n, channels), jnp.bfloat16),
            pltpu.VMEM((2 * rows, lanes), jnp.float32),
            pltpu.SMEM((rows,), jnp.int32),
            pltpu.SMEM((rows,), jnp.int32),
            pltpu.SemaphoreType.DMA((9 + rows,)),
            pltpu.SemaphoreType.DMA,
            pltpu.SemaphoreType.DMA((chips,)),
            pltpu.SemaphoreType.DMA((2,)),
            pltpu.SemaphoreType.DMA((2,)),
            pltpu.SemaphoreType.DMA,
            pltpu.SemaphoreType.DMA,
        ],
        compiler_params=pltpu.CompilerParams(
            collective_id=0, has_side_effects=True, vmem_limit_bytes=60 * 1024 * 1024
        ),
        name="attend",
    )(
        pair_map,
        norm_gain.reshape(1, channels),
        w_query,
        w_key,
        w_value,
        w_gate,
        w_bias.T,
        w_output,
        window_start,
        key_length,
    )


def solution(mesh):
    return jax.shard_map(
        functools.partial(local, mesh.shape["row"]),
        mesh=mesh,
        in_specs=(
            P(("grp", "row"), None, None),
            P(),
            P(),
            P(),
            P(),
            P(),
            P(),
            P(),
            P(("grp", "row")),
            P(("grp", "row")),
        ),
        out_specs=P("grp", "row", None),
        check_vma=False,
    )
```

```python
import functools
import math

import jax
import jax.numpy as jnp
from jax import lax
from jax.experimental import pallas as pl
from jax.experimental.pallas import tpu as pltpu
from jax.sharding import PartitionSpec as P

H = 4
LOG2E = math.log2(math.e)
MESH = pl.DeviceIdType.MESH
NT = (((1,), (1,)), ((), ()))
TN = (((0,), (0,)), ((), ()))
PIECES = 1


def other(index, step, count):
    result, bit = 0, 1
    while bit < count:
        a, b = index // bit % 2, step // bit % 2
        result = result + (a + b - 2 * a * b) * bit
        bit *= 2
    return result


def kernel(
    n,
    x_hbm,
    gain_hbm,
    wq_hbm,
    wk_hbm,
    wv_hbm,
    wg_hbm,
    wb_hbm,
    wo_hbm,
    start_hbm,
    length_hbm,
    out_ref,
    x_ref,
    gain_ref,
    asking_ref,
    giving_ref,
    wb_ref,
    wo_ref,
    bias_ref,
    turned_ref,
    score_ref,
    query_ref,
    key_ref,
    value_ref,
    sig_ref,
    send_ref,
    bound_ref,
    start_ref,
    length_ref,
    in_sem,
    bias_send,
    bias_recv,
    pass_send,
    mate_send,
    mate_recv,
    out_send,
    out_recv,
):
    both, width, channels = x_ref.shape
    rows = both // 2
    head = channels // H
    chips = n // 2
    half = chips // 2
    lanes = H * 4 * rows
    unrolled = chips <= 8
    me = lax.axis_index("row")
    core, chip = me % 2, me // 2
    mate = me + 1 - 2 * core
    place_of_me = lax.rem(me, chips)
    own = core * chips + (1 - core) * place_of_me
    quarter = half // 2
    side = chip // half
    asked_half = side + core - 2 * side * core
    piece = max(1, rows // PIECES)

    def load(source, target, slot):
        copy = pltpu.make_async_copy(source, target, in_sem.at[slot])
        copy.start()
        return copy

    x_in = [
        load(x_hbm.at[pl.ds(at, piece)], x_ref.at[pl.ds(core * rows + at, piece)], 9 + at)
        for at in range(0, rows, piece)
    ]
    first_in = [load(gain_hbm, gain_ref, 0), load(wb_hbm, wb_ref, 1)]
    barrier = pltpu.get_barrier_semaphore()

    def hello(target):
        pl.semaphore_signal(barrier, inc=1, device_id={"row": target}, device_id_type=MESH)

    def greet(at, carry):
        step = chips - 1 - at
        peer = other(chip, step, chips) * 2
        away = step // half
        hello(peer + away)

        @pl.when((core == away) | (step == 1))
        def _():
            hello(peer + 1 - away)

        return carry

    lax.fori_loop(0, chips - 1, greet, 0, unroll=unrolled)
    hello(mate)

    left, right = pl.ds(0, channels), pl.ds(channels, channels)
    window_in = [load(start_hbm, start_ref, 2), load(length_hbm, length_ref, 3)]
    weights_in = [
        load(source, target, 4 + at)
        for at, (source, target) in enumerate(
            (
                (wq_hbm, asking_ref.at[:, left]),
                (wg_hbm, asking_ref.at[:, right]),
                (wk_hbm, giving_ref.at[:, left]),
                (wv_hbm, giving_ref.at[:, right]),
                (wo_hbm, wo_ref),
            )
        )
    ]

    for copy in first_in:
        copy.wait()
    bias_weight = wb_ref[...]
    gain = gain_ref[...]
    ones = jnp.ones((channels, channels), jnp.bfloat16)
    for i in range(rows):
        if i % piece == 0:
            x_in[i // piece].wait()
        row = x_ref[core * rows + i]
        center = jnp.dot(row, ones, preferred_element_type=jnp.float32) * (1.0 / channels)
        values = row.astype(jnp.float32) - center
        spread = jnp.mean(values * values, axis=-1, keepdims=True)
        row = (values * lax.rsqrt(spread + 1e-05) * gain).astype(jnp.bfloat16)
        x_ref[core * rows + i] = row
        local = lax.dot_general(bias_weight, row, NT, preferred_element_type=jnp.float32)
        local = local * LOG2E
        for h in range(H):
            bias_ref[own, h, i : i + 1, :] = local[h : h + 1]
    for copy in window_in:
        copy.wait()
    second = lax.broadcasted_iota(jnp.int32, (1, lanes), 1) // (lanes // 2) == 1
    bounds = []
    for i in range(0, rows, 2):
        first = jnp.where(second, start_ref[i + 1], start_ref[i])
        count = jnp.where(second, length_ref[i + 1], length_ref[i])
        bounds += [first, first + count]
    own_bounds = pl.ds(pl.multiple_of(core * rows, rows), rows)
    bound_ref[own_bounds, :] = jnp.concatenate(bounds, axis=0).astype(jnp.float32)

    pl.semaphore_wait(barrier, 3 * half - 1 + 2 * core)

    def bias_copy(place, target):
        return pltpu.make_async_remote_copy(
            src_ref=bias_ref.at[own],
            dst_ref=bias_ref.at[place],
            send_sem=bias_send,
            recv_sem=bias_recv.at[place],
            device_id={"row": target},
            device_id_type=MESH,
        )

    def mate_copy(ref, slot):
        return pltpu.make_async_remote_copy(
            src_ref=ref.at[own_bounds],
            dst_ref=ref.at[own_bounds],
            send_sem=mate_send.at[slot],
            recv_sem=mate_recv.at[slot],
            device_id={"row": mate},
            device_id_type=MESH,
        )

    def far(step):
        late = step // quarter
        return other(chip, half + 2 * (step - quarter * late) + late, chips)

    def send_far(step, carry):
        bias_copy(place_of_me, far(step) * 2 + 1).start()
        return carry

    def send_near(step, carry):
        bias_copy(place_of_me, other(chip, step, chips) * 2).start()
        return carry

    def pass_on(place):
        return pltpu.make_async_remote_copy(
            src_ref=bias_ref.at[place],
            dst_ref=bias_ref.at[place],
            send_sem=pass_send,
            recv_sem=bias_recv.at[place],
            device_id={"row": other(chip, 1, chips) * 2 + 1},
            device_id_type=MESH,
        )

    x_copy, bound_copy = mate_copy(x_ref, 0), mate_copy(bound_ref, 1)
    lax.fori_loop(0, quarter, send_far, 0, unroll=unrolled)
    x_copy.start()
    bound_copy.start()
    lax.fori_loop(1, half, send_near, 0, unroll=unrolled)

    @pl.when(core == 1)
    def _():
        bias_copy(place_of_me, mate).start()

    for copy in weights_in:
        copy.wait()
    lane = lax.broadcasted_iota(jnp.int32, (1, channels), 1) // head
    masks = [(lane == h).astype(jnp.float32).astype(jnp.bfloat16) for h in range(H)]
    factor = LOG2E / head**0.5

    def project(i, couple, side):
        row = x_ref[i]
        asking = x_ref[i, pl.ds(pl.multiple_of(asked_half * (width // 2), width // 2), width // 2), :]
        asked = jnp.dot(asking, asking_ref[...], preferred_element_type=jnp.float32)
        query_ref[i] = asked[:, :channels].astype(jnp.bfloat16)
        gate = asked[:, channels:].astype(jnp.bfloat16).astype(jnp.float32)
        sig_ref[i] = jax.nn.sigmoid(gate)
        given = jnp.dot(row, giving_ref[...], preferred_element_type=jnp.float32)
        given = given.astype(jnp.bfloat16)
        span = slice(side * channels, (side + 1) * channels)
        key_ref[couple, :, span] = given[:, :channels]
        value_ref[couple, :, span] = given[:, channels:]

    spot = lax.broadcasted_iota(jnp.int32, (width, lanes), 0).astype(jnp.float32)
    wide = 2 * rows
    nothing = jnp.zeros((wide, channels), jnp.bfloat16)

    def score(couple):
        first = bound_ref[pl.ds(2 * couple, 1), :]
        last = bound_ref[pl.ds(2 * couple + 1, 1), :]
        valid = (spot >= first) & (spot < last)
        keys = key_ref[couple]
        for at in range(half):
            queries = [query_ref[2 * couple + side, at * wide : (at + 1) * wide, :] for side in range(2)]
            spread_out = [jnp.concatenate([queries[0] * m, nothing], axis=1) for m in masks]
            spread_out += [jnp.concatenate([nothing, queries[1] * m], axis=1) for m in masks]
            part = lax.dot_general(
                keys, jnp.concatenate(spread_out, axis=0), NT, preferred_element_type=jnp.float32
            )
            score_ref[at, couple] = jnp.where(valid, part * factor, jnp.float32(-1e30))

    def prepare(which):
        first = which * (rows // 2)
        if width <= 128:
            for at in range(rows):
                project(which * rows + at, first + at // 2, at % 2)
            for at in range(rows // 2):
                score(first + at)
        else:

            @pl.loop(0, rows // 2)
            def _(at):
                for side in range(2):
                    project(which * rows + 2 * at + side, first + at, side)
                score(first + at)

    @pl.loop(0, 2)
    def _(turn_at):
        @pl.when(turn_at == 1)
        def _():
            x_copy.wait_recv()
            bound_copy.wait_recv()

        prepare(core + turn_at - 2 * core * turn_at)

    def turn(at):
        blocks = []
        for h in range(H):
            blocks += [bias_ref[at * 2, h], bias_ref[at * 2 + 1, h]]
        turned_ref[...] = jnp.concatenate(blocks * 2, axis=0).T

    def attend(place, couple):
        t = score_ref[place, couple] + turned_ref[...]
        raised = jnp.exp2(t - jnp.max(t, axis=0, keepdims=True))
        total = jnp.sum(raised, axis=0, keepdims=True)
        weights = (raised * (1.0 / total)).astype(jnp.bfloat16).T
        columns = pl.ds(pl.multiple_of(place * wide, wide), wide)
        results = []
        for side in range(2):
            mixed = jnp.dot(
                weights[side * (lanes // 2) : (side + 1) * (lanes // 2)],
                value_ref[couple, :, side * channels : (side + 1) * channels],
                preferred_element_type=jnp.float32,
            )
            attended = mixed[:wide]
            for h in range(1, H):
                attended = jnp.where(lane == h, mixed[h * wide : (h + 1) * wide], attended)
            gated = sig_ref[2 * couple + side, columns, :] * attended
            results.append(gated.astype(jnp.bfloat16))
        return results

    def out_copy(target, part):
        return pltpu.make_async_remote_copy(
            src_ref=send_ref.at[lax.rem(target, chips), pl.ds(part * rows, rows)],
            dst_ref=out_ref.at[pl.ds(pl.multiple_of(chip * both + part * rows, rows), rows)],
            send_sem=out_send,
            recv_sem=out_recv,
            device_id={"row": target},
            device_id_type=MESH,
        )

    def finish(peer, part):
        place = lax.rem(peer, half)
        gated = []
        for at in range(rows // 2):
            gated += attend(place, part * (rows // 2) + at)
        update = jnp.dot(
            jnp.concatenate(gated, axis=0), wo_ref[...], preferred_element_type=jnp.float32
        ).reshape(rows, 2, rows, channels)
        slab = pl.ds(pl.multiple_of(part * rows, rows), rows)
        for q in range(2):
            target = peer * 2 + q
            send_ref[place * 2 + q, slab] = update[:, q].astype(jnp.bfloat16)

            @pl.when(target != me)
            def _():
                out_copy(target, part).start()

            @pl.when(target == me)
            def _():
                here = pl.ds(pl.multiple_of(chip * both + part * rows, rows), rows)
                out_ref[here] = send_ref[place * 2 + q, slab]

    def peer_at(step):
        return core * far(step) + (1 - core) * other(chip, half - 1 - step, chips)

    def take(step):
        peer = peer_at(step)
        for q in range(2):
            place = lax.rem(peer, half) * 2 + q

            @pl.when(peer * 2 + q != me)
            def _():
                bias_copy(place, mate).wait_recv()

            @pl.when((core == 1) & (step < quarter))
            def _():
                pass_on(place).start()

    @pl.loop(0, half)
    def _(step):
        take(step)
        peer = peer_at(step)
        turn(lax.rem(peer, half))
        pl.loop(0, 2)(lambda part: finish(peer, part))

    x_copy.wait_send()
    bound_copy.wait_send()
    def bias_rest(count, send_sem):
        return pltpu.make_async_remote_copy(
            src_ref=bias_ref.at[pl.ds(0, count)],
            dst_ref=bias_ref.at[pl.ds(0, count)],
            send_sem=send_sem,
            recv_sem=bias_recv.at[0],
            device_id={"row": mate},
            device_id_type=MESH,
        )

    def out_rest(count):
        return pltpu.make_async_remote_copy(
            src_ref=send_ref.at[pl.ds(0, count)],
            dst_ref=out_ref.at[pl.ds(0, count * both)],
            send_sem=out_send,
            recv_sem=out_recv,
            device_id={"row": mate},
            device_id_type=MESH,
        )

    for count, which in ((chips - 1, 0), (chips, 1)):

        @pl.when(core == which)
        def _():
            bias_rest(quarter + half - 1 + which, bias_send).wait_send()
            out_rest(count).wait_send()
            out_rest(count).wait_recv()

    @pl.when(core == 1)
    def _():
        bias_rest(half, pass_send).wait_send()


def local(
    n, pair_map, norm_gain, w_query, w_key, w_value, w_gate, w_bias, w_output, window_start, key_length
):
    rows, width, channels = pair_map.shape
    chips = n // 2
    lanes = H * 4 * rows
    outside = pl.BlockSpec(memory_space=pltpu.HBM)
    return pl.pallas_call(
        functools.partial(kernel, n),
        out_shape=pltpu.VMEM((n * rows, width // n, channels), jnp.bfloat16),
        in_specs=[outside] * 10,
        out_specs=pl.BlockSpec(memory_space=pltpu.VMEM),
        scratch_shapes=[
            pltpu.VMEM((2 * rows, width, channels), jnp.bfloat16),
            pltpu.VMEM((1, channels), jnp.float32),
            pltpu.VMEM((channels, 2 * channels), jnp.bfloat16),
            pltpu.VMEM((channels, 2 * channels), jnp.bfloat16),
            pltpu.VMEM((H, channels), jnp.bfloat16),
            pltpu.VMEM((channels, channels), jnp.bfloat16),
            pltpu.VMEM((chips + 1, H, rows, width), jnp.float32),
            pltpu.VMEM((width, lanes), jnp.float32),
            pltpu.VMEM((chips // 2, rows, width, lanes), jnp.float32),
            pltpu.VMEM((2 * rows, width // 2, channels), jnp.bfloat16),
            pltpu.VMEM((rows, width, 2 * channels), jnp.bfloat16),
            pltpu.VMEM((rows, width, 2 * channels), jnp.bfloat16),
            pltpu.VMEM((2 * rows, width // 2, channels), jnp.float32),
            pltpu.VMEM((chips, 2 * rows, width // n, channels), jnp.bfloat16),
            pltpu.VMEM((2 * rows, lanes), jnp.float32),
            pltpu.SMEM((rows,), jnp.int32),
            pltpu.SMEM((rows,), jnp.int32),
            pltpu.SemaphoreType.DMA((9 + rows,)),
            pltpu.SemaphoreType.DMA,
            pltpu.SemaphoreType.DMA((chips,)),
            pltpu.SemaphoreType.DMA,
            pltpu.SemaphoreType.DMA((2,)),
            pltpu.SemaphoreType.DMA((2,)),
            pltpu.SemaphoreType.DMA,
            pltpu.SemaphoreType.DMA,
        ],
        compiler_params=pltpu.CompilerParams(
            collective_id=0, has_side_effects=True, vmem_limit_bytes=60 * 1024 * 1024
        ),
        name="attend",
    )(
        pair_map,
        norm_gain.reshape(1, channels),
        w_query,
        w_key,
        w_value,
        w_gate,
        w_bias.T,
        w_output,
        window_start,
        key_length,
    )


def solution(mesh):
    return jax.shard_map(
        functools.partial(local, mesh.shape["row"]),
        mesh=mesh,
        in_specs=(
            P(("grp", "row"), None, None),
            P(),
            P(),
            P(),
            P(),
            P(),
            P(),
            P(),
            P(("grp", "row")),
            P(("grp", "row")),
        ),
        out_specs=P("grp", "row", None),
        check_vma=False,
    )
```

```python
import functools
import math

import jax
import jax.numpy as jnp
from jax import lax
from jax.experimental import pallas as pl
from jax.experimental.pallas import tpu as pltpu
from jax.sharding import PartitionSpec as P

H = 4
LOG2E = math.log2(math.e)
MESH = pl.DeviceIdType.MESH
NT = (((1,), (1,)), ((), ()))
TN = (((0,), (0,)), ((), ()))
PIECES = 1


def other(index, step, count):
    result, bit = 0, 1
    while bit < count:
        a, b = index // bit % 2, step // bit % 2
        result = result + (a + b - 2 * a * b) * bit
        bit *= 2
    return result


def kernel(
    n,
    x_hbm,
    gain_hbm,
    wq_hbm,
    wk_hbm,
    wv_hbm,
    wg_hbm,
    wb_hbm,
    wo_hbm,
    start_hbm,
    length_hbm,
    out_ref,
    x_ref,
    gain_ref,
    asking_ref,
    giving_ref,
    wb_ref,
    wo_ref,
    bias_ref,
    turned_ref,
    score_ref,
    query_ref,
    key_ref,
    value_ref,
    sig_ref,
    send_ref,
    bound_ref,
    start_ref,
    length_ref,
    in_sem,
    bias_send,
    bias_recv,
    pass_send,
    mate_send,
    mate_recv,
    out_send,
    out_recv,
):
    both, width, channels = x_ref.shape
    rows = both // 2
    head = channels // H
    chips = n // 2
    half = chips // 2
    lanes = H * 4 * rows
    unrolled = chips <= 8
    me = lax.axis_index("row")
    core, chip = me % 2, me // 2
    mate = me + 1 - 2 * core
    place_of_me = lax.rem(me, chips)
    own = core * chips + (1 - core) * place_of_me
    quarter = half // 2
    side = chip // half
    asked_half = side + core - 2 * side * core
    piece = max(1, rows // PIECES)

    def load(source, target, slot):
        copy = pltpu.make_async_copy(source, target, in_sem.at[slot])
        copy.start()
        return copy

    x_in = [
        load(x_hbm.at[pl.ds(at, piece)], x_ref.at[pl.ds(core * rows + at, piece)], 9 + at)
        for at in range(0, rows, piece)
    ]
    first_in = [load(gain_hbm, gain_ref, 0), load(wb_hbm, wb_ref, 1)]
    barrier = pltpu.get_barrier_semaphore()

    def hello(target):
        pl.semaphore_signal(barrier, inc=1, device_id={"row": target}, device_id_type=MESH)

    def greet(step, carry):
        peer = other(chip, step, chips) * 2
        away = step // half
        hello(peer + away)

        @pl.when((core == away) | (step == 1))
        def _():
            hello(peer + 1 - away)

        return carry

    def greet_far(at, carry):
        return greet(chips - 2 - 2 * at, carry)

    lax.fori_loop(0, quarter, greet_far, 0, unroll=unrolled)
    lax.fori_loop(1, half, greet, 0, unroll=unrolled)
    hello(mate)

    left, right = pl.ds(0, channels), pl.ds(channels, channels)
    window_in = [load(start_hbm, start_ref, 2), load(length_hbm, length_ref, 3)]
    weights_in = [
        load(source, target, 4 + at)
        for at, (source, target) in enumerate(
            (
                (wq_hbm, asking_ref.at[:, left]),
                (wg_hbm, asking_ref.at[:, right]),
                (wk_hbm, giving_ref.at[:, left]),
                (wv_hbm, giving_ref.at[:, right]),
                (wo_hbm, wo_ref),
            )
        )
    ]

    for copy in first_in:
        copy.wait()
    bias_weight = wb_ref[...]
    gain = gain_ref[...]
    ones = jnp.ones((channels, channels), jnp.bfloat16)
    for i in range(rows):
        if i % piece == 0:
            x_in[i // piece].wait()
        row = x_ref[core * rows + i]
        center = jnp.dot(row, ones, preferred_element_type=jnp.float32) * (1.0 / channels)
        values = row.astype(jnp.float32) - center
        spread = jnp.mean(values * values, axis=-1, keepdims=True)
        row = (values * lax.rsqrt(spread + 1e-05) * gain).astype(jnp.bfloat16)
        x_ref[core * rows + i] = row
        local = lax.dot_general(bias_weight, row, NT, preferred_element_type=jnp.float32)
        local = local * LOG2E
        for h in range(H):
            bias_ref[own, h, i : i + 1, :] = local[h : h + 1]
    for copy in window_in:
        copy.wait()
    second = lax.broadcasted_iota(jnp.int32, (1, lanes), 1) // (lanes // 2) == 1
    bounds = []
    for i in range(0, rows, 2):
        first = jnp.where(second, start_ref[i + 1], start_ref[i])
        count = jnp.where(second, length_ref[i + 1], length_ref[i])
        bounds += [first, first + count]
    own_bounds = pl.ds(pl.multiple_of(core * rows, rows), rows)
    bound_ref[own_bounds, :] = jnp.concatenate(bounds, axis=0).astype(jnp.float32)

    pl.semaphore_wait(barrier, quarter + 2 * half - 1 - core * (quarter - 2))

    def bias_copy(place, target):
        return pltpu.make_async_remote_copy(
            src_ref=bias_ref.at[own],
            dst_ref=bias_ref.at[place],
            send_sem=bias_send,
            recv_sem=bias_recv.at[place],
            device_id={"row": target},
            device_id_type=MESH,
        )

    def mate_copy(ref, slot):
        return pltpu.make_async_remote_copy(
            src_ref=ref.at[own_bounds],
            dst_ref=ref.at[own_bounds],
            send_sem=mate_send.at[slot],
            recv_sem=mate_recv.at[slot],
            device_id={"row": mate},
            device_id_type=MESH,
        )

    def far(step):
        late = step // quarter
        return other(chip, half + 2 * (step - quarter * late) + late, chips)

    def send_far(step, carry):
        bias_copy(place_of_me, far(step) * 2 + 1).start()
        return carry

    def send_near(step, carry):
        bias_copy(place_of_me, other(chip, step, chips) * 2).start()
        return carry

    def pass_on(place):
        return pltpu.make_async_remote_copy(
            src_ref=bias_ref.at[place],
            dst_ref=bias_ref.at[place],
            send_sem=pass_send,
            recv_sem=bias_recv.at[place],
            device_id={"row": other(chip, 1, chips) * 2 + 1},
            device_id_type=MESH,
        )

    x_copy, bound_copy = mate_copy(x_ref, 0), mate_copy(bound_ref, 1)
    lax.fori_loop(0, quarter, send_far, 0, unroll=unrolled)
    x_copy.start()
    bound_copy.start()
    lax.fori_loop(1, half, send_near, 0, unroll=unrolled)

    @pl.when(core == 1)
    def _():
        bias_copy(place_of_me, mate).start()

    for copy in weights_in:
        copy.wait()
    lane = lax.broadcasted_iota(jnp.int32, (1, channels), 1) // head
    masks = [(lane == h).astype(jnp.float32).astype(jnp.bfloat16) for h in range(H)]
    factor = LOG2E / head**0.5

    def project(i, couple, side):
        row = x_ref[i]
        asking = x_ref[i, pl.ds(pl.multiple_of(asked_half * (width // 2), width // 2), width // 2), :]
        asked = jnp.dot(asking, asking_ref[...], preferred_element_type=jnp.float32)
        query_ref[i] = asked[:, :channels].astype(jnp.bfloat16)
        gate = asked[:, channels:].astype(jnp.bfloat16).astype(jnp.float32)
        sig_ref[i] = jax.nn.sigmoid(gate)
        given = jnp.dot(row, giving_ref[...], preferred_element_type=jnp.float32)
        given = given.astype(jnp.bfloat16)
        span = slice(side * channels, (side + 1) * channels)
        key_ref[couple, :, span] = given[:, :channels]
        value_ref[couple, :, span] = given[:, channels:]

    spot = lax.broadcasted_iota(jnp.int32, (width, lanes), 0).astype(jnp.float32)
    wide = 2 * rows
    nothing = jnp.zeros((wide, channels), jnp.bfloat16)

    def score(couple):
        first = bound_ref[pl.ds(2 * couple, 1), :]
        last = bound_ref[pl.ds(2 * couple + 1, 1), :]
        valid = (spot >= first) & (spot < last)
        keys = key_ref[couple]
        for at in range(half):
            queries = [query_ref[2 * couple + side, at * wide : (at + 1) * wide, :] for side in range(2)]
            spread_out = [jnp.concatenate([queries[0] * m, nothing], axis=1) for m in masks]
            spread_out += [jnp.concatenate([nothing, queries[1] * m], axis=1) for m in masks]
            part = lax.dot_general(
                keys, jnp.concatenate(spread_out, axis=0), NT, preferred_element_type=jnp.float32
            )
            score_ref[at, couple] = jnp.where(valid, part * factor, jnp.float32(-1e30))

    def prepare(which):
        first = which * (rows // 2)
        if width <= 128:
            for at in range(rows):
                project(which * rows + at, first + at // 2, at % 2)
            for at in range(rows // 2):
                score(first + at)
        else:

            @pl.loop(0, rows // 2)
            def _(at):
                for side in range(2):
                    project(which * rows + 2 * at + side, first + at, side)
                score(first + at)

    @pl.loop(0, 2)
    def _(turn_at):
        @pl.when(turn_at == 1)
        def _():
            x_copy.wait_recv()
            bound_copy.wait_recv()

        prepare(core + turn_at - 2 * core * turn_at)

    def turn(at):
        blocks = []
        for h in range(H):
            blocks += [bias_ref[at * 2, h], bias_ref[at * 2 + 1, h]]
        turned_ref[...] = jnp.concatenate(blocks * 2, axis=0).T

    def attend(place, couple):
        t = score_ref[place, couple] + turned_ref[...]
        raised = jnp.exp2(t - jnp.max(t, axis=0, keepdims=True))
        total = jnp.sum(raised, axis=0, keepdims=True)
        weights = (raised * (1.0 / total)).astype(jnp.bfloat16).T
        columns = pl.ds(pl.multiple_of(place * wide, wide), wide)
        results = []
        for side in range(2):
            mixed = jnp.dot(
                weights[side * (lanes // 2) : (side + 1) * (lanes // 2)],
                value_ref[couple, :, side * channels : (side + 1) * channels],
                preferred_element_type=jnp.float32,
            )
            attended = mixed[:wide]
            for h in range(1, H):
                attended = jnp.where(lane == h, mixed[h * wide : (h + 1) * wide], attended)
            gated = sig_ref[2 * couple + side, columns, :] * attended
            results.append(gated.astype(jnp.bfloat16))
        return results

    def out_copy(target, part):
        return pltpu.make_async_remote_copy(
            src_ref=send_ref.at[lax.rem(target, chips), pl.ds(part * rows, rows)],
            dst_ref=out_ref.at[pl.ds(pl.multiple_of(chip * both + part * rows, rows), rows)],
            send_sem=out_send,
            recv_sem=out_recv,
            device_id={"row": target},
            device_id_type=MESH,
        )

    def finish(peer, part):
        place = lax.rem(peer, half)
        gated = []
        for at in range(rows // 2):
            gated += attend(place, part * (rows // 2) + at)
        update = jnp.dot(
            jnp.concatenate(gated, axis=0), wo_ref[...], preferred_element_type=jnp.float32
        ).reshape(rows, 2, rows, channels)
        slab = pl.ds(pl.multiple_of(part * rows, rows), rows)
        for q in range(2):
            target = peer * 2 + q
            send_ref[place * 2 + q, slab] = update[:, q].astype(jnp.bfloat16)

            @pl.when(target != me)
            def _():
                out_copy(target, part).start()

            @pl.when(target == me)
            def _():
                here = pl.ds(pl.multiple_of(chip * both + part * rows, rows), rows)
                out_ref[here] = send_ref[place * 2 + q, slab]

    def peer_at(step):
        return core * far(step) + (1 - core) * other(chip, half - 1 - step, chips)

    def take(step):
        peer = peer_at(step)
        for q in range(2):
            place = lax.rem(peer, half) * 2 + q

            @pl.when(peer * 2 + q != me)
            def _():
                bias_copy(place, mate).wait_recv()

            @pl.when((core == 1) & (step < quarter))
            def _():
                pass_on(place).start()

    @pl.loop(0, half)
    def _(step):
        take(step)
        peer = peer_at(step)
        turn(lax.rem(peer, half))
        pl.loop(0, 2)(lambda part: finish(peer, part))

    x_copy.wait_send()
    bound_copy.wait_send()
    def bias_rest(count, send_sem):
        return pltpu.make_async_remote_copy(
            src_ref=bias_ref.at[pl.ds(0, count)],
            dst_ref=bias_ref.at[pl.ds(0, count)],
            send_sem=send_sem,
            recv_sem=bias_recv.at[0],
            device_id={"row": mate},
            device_id_type=MESH,
        )

    def out_rest(count):
        return pltpu.make_async_remote_copy(
            src_ref=send_ref.at[pl.ds(0, count)],
            dst_ref=out_ref.at[pl.ds(0, count * both)],
            send_sem=out_send,
            recv_sem=out_recv,
            device_id={"row": mate},
            device_id_type=MESH,
        )

    for count, which in ((chips - 1, 0), (chips, 1)):

        @pl.when(core == which)
        def _():
            bias_rest(quarter + half - 1 + which, bias_send).wait_send()
            out_rest(count).wait_send()
            out_rest(count).wait_recv()

    @pl.when(core == 1)
    def _():
        bias_rest(half, pass_send).wait_send()


def local(
    n, pair_map, norm_gain, w_query, w_key, w_value, w_gate, w_bias, w_output, window_start, key_length
):
    rows, width, channels = pair_map.shape
    chips = n // 2
    lanes = H * 4 * rows
    outside = pl.BlockSpec(memory_space=pltpu.HBM)
    return pl.pallas_call(
        functools.partial(kernel, n),
        out_shape=pltpu.VMEM((n * rows, width // n, channels), jnp.bfloat16),
        in_specs=[outside] * 10,
        out_specs=pl.BlockSpec(memory_space=pltpu.VMEM),
        scratch_shapes=[
            pltpu.VMEM((2 * rows, width, channels), jnp.bfloat16),
            pltpu.VMEM((1, channels), jnp.float32),
            pltpu.VMEM((channels, 2 * channels), jnp.bfloat16),
            pltpu.VMEM((channels, 2 * channels), jnp.bfloat16),
            pltpu.VMEM((H, channels), jnp.bfloat16),
            pltpu.VMEM((channels, channels), jnp.bfloat16),
            pltpu.VMEM((chips + 1, H, rows, width), jnp.float32),
            pltpu.VMEM((width, lanes), jnp.float32),
            pltpu.VMEM((chips // 2, rows, width, lanes), jnp.float32),
            pltpu.VMEM((2 * rows, width // 2, channels), jnp.bfloat16),
            pltpu.VMEM((rows, width, 2 * channels), jnp.bfloat16),
            pltpu.VMEM((rows, width, 2 * channels), jnp.bfloat16),
            pltpu.VMEM((2 * rows, width // 2, channels), jnp.float32),
            pltpu.VMEM((chips, 2 * rows, width // n, channels), jnp.bfloat16),
            pltpu.VMEM((2 * rows, lanes), jnp.float32),
            pltpu.SMEM((rows,), jnp.int32),
            pltpu.SMEM((rows,), jnp.int32),
            pltpu.SemaphoreType.DMA((9 + rows,)),
            pltpu.SemaphoreType.DMA,
            pltpu.SemaphoreType.DMA((chips,)),
            pltpu.SemaphoreType.DMA,
            pltpu.SemaphoreType.DMA((2,)),
            pltpu.SemaphoreType.DMA((2,)),
            pltpu.SemaphoreType.DMA,
            pltpu.SemaphoreType.DMA,
        ],
        compiler_params=pltpu.CompilerParams(
            collective_id=0, has_side_effects=True, vmem_limit_bytes=60 * 1024 * 1024
        ),
        name="attend",
    )(
        pair_map,
        norm_gain.reshape(1, channels),
        w_query,
        w_key,
        w_value,
        w_gate,
        w_bias.T,
        w_output,
        window_start,
        key_length,
    )


def solution(mesh):
    return jax.shard_map(
        functools.partial(local, mesh.shape["row"]),
        mesh=mesh,
        in_specs=(
            P(("grp", "row"), None, None),
            P(),
            P(),
            P(),
            P(),
            P(),
            P(),
            P(),
            P(("grp", "row")),
            P(("grp", "row")),
        ),
        out_specs=P("grp", "row", None),
        check_vma=False,
    )
```

```python
import functools
import math

import jax
import jax.numpy as jnp
from jax import lax
from jax.experimental import pallas as pl
from jax.experimental.pallas import tpu as pltpu
from jax.sharding import PartitionSpec as P

H = 4
LOG2E = math.log2(math.e)
MESH = pl.DeviceIdType.MESH
NT = (((1,), (1,)), ((), ()))
TN = (((0,), (0,)), ((), ()))
PIECES = 1


def other(index, step, count):
    result, bit = 0, 1
    while bit < count:
        a, b = index // bit % 2, step // bit % 2
        result = result + (a + b - 2 * a * b) * bit
        bit *= 2
    return result


def kernel(
    n,
    x_hbm,
    gain_hbm,
    wq_hbm,
    wk_hbm,
    wv_hbm,
    wg_hbm,
    wb_hbm,
    wo_hbm,
    start_hbm,
    length_hbm,
    out_ref,
    x_ref,
    gain_ref,
    asking_ref,
    giving_ref,
    wb_ref,
    wo_ref,
    bias_ref,
    turned_ref,
    score_ref,
    query_ref,
    key_ref,
    value_ref,
    sig_ref,
    send_ref,
    bound_ref,
    start_ref,
    length_ref,
    in_sem,
    bias_send,
    bias_recv,
    pass_send,
    mate_send,
    mate_recv,
    out_send,
    out_recv,
):
    both, width, channels = x_ref.shape
    rows = both // 2
    head = channels // H
    chips = n // 2
    half = chips // 2
    lanes = H * 4 * rows
    unrolled = chips <= 8
    me = lax.axis_index("row")
    core, chip = me % 2, me // 2
    mate = me + 1 - 2 * core
    place_of_me = lax.rem(me, chips)
    own = core * chips + (1 - core) * place_of_me
    quarter = half // 2
    side = chip // half
    asked_half = side + core - 2 * side * core
    piece = max(1, rows // PIECES)

    def load(source, target, slot):
        copy = pltpu.make_async_copy(source, target, in_sem.at[slot])
        copy.start()
        return copy

    x_in = [
        load(x_hbm.at[pl.ds(at, piece)], x_ref.at[pl.ds(core * rows + at, piece)], 9 + at)
        for at in range(0, rows, piece)
    ]
    first_in = [load(gain_hbm, gain_ref, 0), load(wb_hbm, wb_ref, 1)]
    barrier = pltpu.get_barrier_semaphore()

    def hello(target):
        pl.semaphore_signal(barrier, inc=1, device_id={"row": target}, device_id_type=MESH)

    def greet_both(peer, when):
        @pl.when(when)
        def _():
            hello(peer * 2)
            hello(peer * 2 + 1)

    def greet_far(at, carry):
        peer = other(chip, chips - 2 - 2 * at, chips)
        greet_both(peer, core == 1)
        return carry

    def greet_near(step, carry):
        peer = other(chip, step, chips)
        greet_both(peer, core == 0)
        return carry

    lax.fori_loop(0, quarter, greet_far, 0, unroll=unrolled)
    lax.fori_loop(1, half, greet_near, 0, unroll=unrolled)

    @pl.when(core == 1)
    def _():
        hello(other(chip, 1, chips) * 2 + 1)

    hello(mate)

    left, right = pl.ds(0, channels), pl.ds(channels, channels)
    window_in = [load(start_hbm, start_ref, 2), load(length_hbm, length_ref, 3)]
    weights_in = [
        load(source, target, 4 + at)
        for at, (source, target) in enumerate(
            (
                (wq_hbm, asking_ref.at[:, left]),
                (wg_hbm, asking_ref.at[:, right]),
                (wk_hbm, giving_ref.at[:, left]),
                (wv_hbm, giving_ref.at[:, right]),
                (wo_hbm, wo_ref),
            )
        )
    ]

    for copy in first_in:
        copy.wait()
    bias_weight = wb_ref[...]
    gain = gain_ref[...]
    ones = jnp.ones((channels, channels), jnp.bfloat16)
    for i in range(rows):
        if i % piece == 0:
            x_in[i // piece].wait()
        row = x_ref[core * rows + i]
        center = jnp.dot(row, ones, preferred_element_type=jnp.float32) * (1.0 / channels)
        values = row.astype(jnp.float32) - center
        spread = jnp.mean(values * values, axis=-1, keepdims=True)
        row = (values * lax.rsqrt(spread + 1e-05) * gain).astype(jnp.bfloat16)
        x_ref[core * rows + i] = row
        local = lax.dot_general(bias_weight, row, NT, preferred_element_type=jnp.float32)
        local = local * LOG2E
        for h in range(H):
            bias_ref[own, h, i : i + 1, :] = local[h : h + 1]
    for copy in window_in:
        copy.wait()
    second = lax.broadcasted_iota(jnp.int32, (1, lanes), 1) // (lanes // 2) == 1
    bounds = []
    for i in range(0, rows, 2):
        first = jnp.where(second, start_ref[i + 1], start_ref[i])
        count = jnp.where(second, length_ref[i + 1], length_ref[i])
        bounds += [first, first + count]
    own_bounds = pl.ds(pl.multiple_of(core * rows, rows), rows)
    bound_ref[own_bounds, :] = jnp.concatenate(bounds, axis=0).astype(jnp.float32)

    pl.semaphore_wait(barrier, half + core + quarter)

    def bias_copy(place, target):
        return pltpu.make_async_remote_copy(
            src_ref=bias_ref.at[own],
            dst_ref=bias_ref.at[place],
            send_sem=bias_send,
            recv_sem=bias_recv.at[place],
            device_id={"row": target},
            device_id_type=MESH,
        )

    def mate_copy(ref, slot):
        return pltpu.make_async_remote_copy(
            src_ref=ref.at[own_bounds],
            dst_ref=ref.at[own_bounds],
            send_sem=mate_send.at[slot],
            recv_sem=mate_recv.at[slot],
            device_id={"row": mate},
            device_id_type=MESH,
        )

    def far(step):
        late = step // quarter
        return other(chip, chips - 2 - 2 * (step - quarter * late) + late, chips)

    def send_far(step, carry):
        bias_copy(place_of_me, far(step) * 2 + 1).start()
        return carry

    def send_near(step, carry):
        bias_copy(place_of_me, other(chip, step, chips) * 2).start()
        return carry

    def pass_on(place):
        return pltpu.make_async_remote_copy(
            src_ref=bias_ref.at[place],
            dst_ref=bias_ref.at[place],
            send_sem=pass_send,
            recv_sem=bias_recv.at[place],
            device_id={"row": other(chip, 1, chips) * 2 + 1},
            device_id_type=MESH,
        )

    x_copy, bound_copy = mate_copy(x_ref, 0), mate_copy(bound_ref, 1)
    lax.fori_loop(0, quarter, send_far, 0, unroll=unrolled)
    x_copy.start()
    bound_copy.start()
    lax.fori_loop(1, half, send_near, 0, unroll=unrolled)

    @pl.when(core == 1)
    def _():
        bias_copy(place_of_me, mate).start()

    for copy in weights_in:
        copy.wait()
    lane = lax.broadcasted_iota(jnp.int32, (1, channels), 1) // head
    masks = [(lane == h).astype(jnp.float32).astype(jnp.bfloat16) for h in range(H)]
    factor = LOG2E / head**0.5

    def project(i, couple, side):
        row = x_ref[i]
        asking = x_ref[i, pl.ds(pl.multiple_of(asked_half * (width // 2), width // 2), width // 2), :]
        asked = jnp.dot(asking, asking_ref[...], preferred_element_type=jnp.float32)
        query_ref[i] = asked[:, :channels].astype(jnp.bfloat16)
        gate = asked[:, channels:].astype(jnp.bfloat16).astype(jnp.float32)
        sig_ref[i] = jax.nn.sigmoid(gate)
        given = jnp.dot(row, giving_ref[...], preferred_element_type=jnp.float32)
        given = given.astype(jnp.bfloat16)
        span = slice(side * channels, (side + 1) * channels)
        key_ref[couple, :, span] = given[:, :channels]
        value_ref[couple, :, span] = given[:, channels:]

    spot = lax.broadcasted_iota(jnp.int32, (width, lanes), 0).astype(jnp.float32)
    wide = 2 * rows
    nothing = jnp.zeros((wide, channels), jnp.bfloat16)

    def score(couple):
        first = bound_ref[pl.ds(2 * couple, 1), :]
        last = bound_ref[pl.ds(2 * couple + 1, 1), :]
        valid = (spot >= first) & (spot < last)
        keys = key_ref[couple]
        for at in range(half):
            queries = [query_ref[2 * couple + side, at * wide : (at + 1) * wide, :] for side in range(2)]
            spread_out = [jnp.concatenate([queries[0] * m, nothing], axis=1) for m in masks]
            spread_out += [jnp.concatenate([nothing, queries[1] * m], axis=1) for m in masks]
            part = lax.dot_general(
                keys, jnp.concatenate(spread_out, axis=0), NT, preferred_element_type=jnp.float32
            )
            score_ref[at, couple] = jnp.where(valid, part * factor, jnp.float32(-1e30))

    def prepare(which):
        first = which * (rows // 2)
        if width <= 128:
            for at in range(rows):
                project(which * rows + at, first + at // 2, at % 2)
            for at in range(rows // 2):
                score(first + at)
        else:

            @pl.loop(0, rows // 2)
            def _(at):
                for side in range(2):
                    project(which * rows + 2 * at + side, first + at, side)
                score(first + at)

    @pl.loop(0, 2)
    def _(turn_at):
        @pl.when(turn_at == 1)
        def _():
            x_copy.wait_recv()
            bound_copy.wait_recv()

        prepare(core + turn_at - 2 * core * turn_at)

    def turn(at):
        blocks = []
        for h in range(H):
            blocks += [bias_ref[at * 2, h], bias_ref[at * 2 + 1, h]]
        turned_ref[...] = jnp.concatenate(blocks * 2, axis=0).T

    def attend(place, couple):
        t = score_ref[place, couple] + turned_ref[...]
        raised = jnp.exp2(t - jnp.max(t, axis=0, keepdims=True))
        total = jnp.sum(raised, axis=0, keepdims=True)
        weights = (raised * (1.0 / total)).astype(jnp.bfloat16).T
        columns = pl.ds(pl.multiple_of(place * wide, wide), wide)
        results = []
        for side in range(2):
            mixed = jnp.dot(
                weights[side * (lanes // 2) : (side + 1) * (lanes // 2)],
                value_ref[couple, :, side * channels : (side + 1) * channels],
                preferred_element_type=jnp.float32,
            )
            attended = mixed[:wide]
            for h in range(1, H):
                attended = jnp.where(lane == h, mixed[h * wide : (h + 1) * wide], attended)
            gated = sig_ref[2 * couple + side, columns, :] * attended
            results.append(gated.astype(jnp.bfloat16))
        return results

    def out_copy(target, part):
        return pltpu.make_async_remote_copy(
            src_ref=send_ref.at[lax.rem(target, chips), pl.ds(part * rows, rows)],
            dst_ref=out_ref.at[pl.ds(pl.multiple_of(chip * both + part * rows, rows), rows)],
            send_sem=out_send,
            recv_sem=out_recv,
            device_id={"row": target},
            device_id_type=MESH,
        )

    def finish(peer, part):
        place = lax.rem(peer, half)
        gated = []
        for at in range(rows // 2):
            gated += attend(place, part * (rows // 2) + at)
        update = jnp.dot(
            jnp.concatenate(gated, axis=0), wo_ref[...], preferred_element_type=jnp.float32
        ).reshape(rows, 2, rows, channels)
        slab = pl.ds(pl.multiple_of(part * rows, rows), rows)
        for q in range(2):
            target = peer * 2 + q
            send_ref[place * 2 + q, slab] = update[:, q].astype(jnp.bfloat16)

            @pl.when(target != me)
            def _():
                out_copy(target, part).start()

            @pl.when(target == me)
            def _():
                here = pl.ds(pl.multiple_of(chip * both + part * rows, rows), rows)
                out_ref[here] = send_ref[place * 2 + q, slab]

    def peer_at(step):
        return core * far(step) + (1 - core) * other(chip, half - 1 - step, chips)

    def take(step):
        peer = peer_at(step)
        for q in range(2):
            place = lax.rem(peer, half) * 2 + q

            @pl.when(peer * 2 + q != me)
            def _():
                bias_copy(place, mate).wait_recv()

            @pl.when((core == 1) & (step < quarter))
            def _():
                pass_on(place).start()

    @pl.loop(0, half)
    def _(step):
        take(step)
        peer = peer_at(step)
        turn(lax.rem(peer, half))
        pl.loop(0, 2)(lambda part: finish(peer, part))

    x_copy.wait_send()
    bound_copy.wait_send()
    def bias_rest(count, send_sem):
        return pltpu.make_async_remote_copy(
            src_ref=bias_ref.at[pl.ds(0, count)],
            dst_ref=bias_ref.at[pl.ds(0, count)],
            send_sem=send_sem,
            recv_sem=bias_recv.at[0],
            device_id={"row": mate},
            device_id_type=MESH,
        )

    def out_rest(count):
        return pltpu.make_async_remote_copy(
            src_ref=send_ref.at[pl.ds(0, count)],
            dst_ref=out_ref.at[pl.ds(0, count * both)],
            send_sem=out_send,
            recv_sem=out_recv,
            device_id={"row": mate},
            device_id_type=MESH,
        )

    for count, which in ((chips - 1, 0), (chips, 1)):

        @pl.when(core == which)
        def _():
            bias_rest(quarter + half - 1 + which, bias_send).wait_send()
            out_rest(count).wait_send()
            out_rest(count).wait_recv()

    @pl.when(core == 1)
    def _():
        bias_rest(half, pass_send).wait_send()


def local(
    n, pair_map, norm_gain, w_query, w_key, w_value, w_gate, w_bias, w_output, window_start, key_length
):
    rows, width, channels = pair_map.shape
    chips = n // 2
    lanes = H * 4 * rows
    outside = pl.BlockSpec(memory_space=pltpu.HBM)
    return pl.pallas_call(
        functools.partial(kernel, n),
        out_shape=pltpu.VMEM((n * rows, width // n, channels), jnp.bfloat16),
        in_specs=[outside] * 10,
        out_specs=pl.BlockSpec(memory_space=pltpu.VMEM),
        scratch_shapes=[
            pltpu.VMEM((2 * rows, width, channels), jnp.bfloat16),
            pltpu.VMEM((1, channels), jnp.float32),
            pltpu.VMEM((channels, 2 * channels), jnp.bfloat16),
            pltpu.VMEM((channels, 2 * channels), jnp.bfloat16),
            pltpu.VMEM((H, channels), jnp.bfloat16),
            pltpu.VMEM((channels, channels), jnp.bfloat16),
            pltpu.VMEM((chips + 1, H, rows, width), jnp.float32),
            pltpu.VMEM((width, lanes), jnp.float32),
            pltpu.VMEM((chips // 2, rows, width, lanes), jnp.float32),
            pltpu.VMEM((2 * rows, width // 2, channels), jnp.bfloat16),
            pltpu.VMEM((rows, width, 2 * channels), jnp.bfloat16),
            pltpu.VMEM((rows, width, 2 * channels), jnp.bfloat16),
            pltpu.VMEM((2 * rows, width // 2, channels), jnp.float32),
            pltpu.VMEM((chips, 2 * rows, width // n, channels), jnp.bfloat16),
            pltpu.VMEM((2 * rows, lanes), jnp.float32),
            pltpu.SMEM((rows,), jnp.int32),
            pltpu.SMEM((rows,), jnp.int32),
            pltpu.SemaphoreType.DMA((9 + rows,)),
            pltpu.SemaphoreType.DMA,
            pltpu.SemaphoreType.DMA((chips,)),
            pltpu.SemaphoreType.DMA,
            pltpu.SemaphoreType.DMA((2,)),
            pltpu.SemaphoreType.DMA((2,)),
            pltpu.SemaphoreType.DMA,
            pltpu.SemaphoreType.DMA,
        ],
        compiler_params=pltpu.CompilerParams(
            collective_id=0, has_side_effects=True, vmem_limit_bytes=60 * 1024 * 1024
        ),
        name="attend",
    )(
        pair_map,
        norm_gain.reshape(1, channels),
        w_query,
        w_key,
        w_value,
        w_gate,
        w_bias.T,
        w_output,
        window_start,
        key_length,
    )


def solution(mesh):
    return jax.shard_map(
        functools.partial(local, mesh.shape["row"]),
        mesh=mesh,
        in_specs=(
            P(("grp", "row"), None, None),
            P(),
            P(),
            P(),
            P(),
            P(),
            P(),
            P(),
            P(("grp", "row")),
            P(("grp", "row")),
        ),
        out_specs=P("grp", "row", None),
        check_vma=False,
    )
```

```python
import functools
import math

import jax
import jax.numpy as jnp
from jax import lax
from jax.experimental import pallas as pl
from jax.experimental.pallas import tpu as pltpu
from jax.sharding import PartitionSpec as P

H = 4
LOG2E = math.log2(math.e)
MESH = pl.DeviceIdType.MESH
NT = (((1,), (1,)), ((), ()))
TN = (((0,), (0,)), ((), ()))
PIECES = 1


def other(index, step, count):
    result, bit = 0, 1
    while bit < count:
        a, b = index // bit % 2, step // bit % 2
        result = result + (a + b - 2 * a * b) * bit
        bit *= 2
    return result


def kernel(
    n,
    x_hbm,
    gain_hbm,
    wq_hbm,
    wk_hbm,
    wv_hbm,
    wg_hbm,
    wb_hbm,
    wo_hbm,
    start_hbm,
    length_hbm,
    out_ref,
    x_ref,
    gain_ref,
    asking_ref,
    giving_ref,
    wb_ref,
    wo_ref,
    bias_ref,
    turned_ref,
    score_ref,
    query_ref,
    key_ref,
    value_ref,
    sig_ref,
    send_ref,
    bound_ref,
    start_ref,
    length_ref,
    in_sem,
    bias_send,
    bias_recv,
    pass_send,
    mate_send,
    mate_recv,
    out_send,
    out_recv,
):
    both, width, channels = x_ref.shape
    rows = both // 2
    head = channels // H
    chips = n // 2
    half = chips // 2
    lanes = H * 4 * rows
    unrolled = chips <= 8
    me = lax.axis_index("row")
    core, chip = me % 2, me // 2
    mate = me + 1 - 2 * core
    place_of_me = lax.rem(me, chips)
    own = core * chips + (1 - core) * place_of_me
    quarter = half // 2
    side = chip // half
    asked_half = side + core - 2 * side * core
    piece = max(1, rows // PIECES)

    def load(source, target, slot):
        copy = pltpu.make_async_copy(source, target, in_sem.at[slot])
        copy.start()
        return copy

    barrier = pltpu.get_barrier_semaphore()

    def hello(target):
        pl.semaphore_signal(barrier, inc=1, device_id={"row": target}, device_id_type=MESH)

    def greet_both(peer, when):
        @pl.when(when)
        def _():
            hello(peer * 2)
            hello(peer * 2 + 1)

    def greet_far(at, carry):
        peer = other(chip, chips - 2 - 2 * at, chips)
        greet_both(peer, core == 1)
        return carry

    def greet_near(step, carry):
        peer = other(chip, step, chips)
        greet_both(peer, core == 0)
        return carry

    lax.fori_loop(0, quarter, greet_far, 0, unroll=unrolled)
    lax.fori_loop(1, half, greet_near, 0, unroll=unrolled)

    @pl.when(core == 1)
    def _():
        hello(other(chip, 1, chips) * 2 + 1)

    hello(mate)

    x_in = [
        load(x_hbm.at[pl.ds(at, piece)], x_ref.at[pl.ds(core * rows + at, piece)], 9 + at // piece)
        for at in range(0, rows, piece)
    ]
    first_in = [load(gain_hbm, gain_ref, 0), load(wb_hbm, wb_ref, 1)]
    left, right = pl.ds(0, channels), pl.ds(channels, channels)
    window_in = [load(start_hbm, start_ref, 2), load(length_hbm, length_ref, 3)]
    weights_in = [
        load(source, target, 4 + at)
        for at, (source, target) in enumerate(
            (
                (wq_hbm, asking_ref.at[:, left]),
                (wg_hbm, asking_ref.at[:, right]),
                (wk_hbm, giving_ref.at[:, left]),
                (wv_hbm, giving_ref.at[:, right]),
                (wo_hbm, wo_ref),
            )
        )
    ]

    for copy in first_in:
        copy.wait()
    bias_weight = wb_ref[...]
    gain = gain_ref[...]
    across = lax.broadcasted_iota(jnp.int32, (channels, channels), 1)
    down = lax.broadcasted_iota(jnp.int32, (channels, channels), 0)
    centring = (across == down).astype(jnp.float32) - 1.0 / channels
    centring = centring.astype(jnp.bfloat16)
    for i in range(rows):
        if i % piece == 0:
            x_in[i // piece].wait()
        row = x_ref[core * rows + i]
        values = jnp.dot(row, centring, preferred_element_type=jnp.float32)
        spread = jnp.mean(values * values, axis=-1, keepdims=True)
        row = (values * lax.rsqrt(spread + 1e-05) * gain).astype(jnp.bfloat16)
        x_ref[core * rows + i] = row
        local = lax.dot_general(bias_weight, row, NT, preferred_element_type=jnp.float32)
        local = local * LOG2E
        for h in range(H):
            bias_ref[own, h, i : i + 1, :] = local[h : h + 1]
    for copy in window_in:
        copy.wait()
    second = lax.broadcasted_iota(jnp.int32, (1, lanes), 1) // (lanes // 2) == 1
    bounds = []
    for i in range(0, rows, 2):
        first = jnp.where(second, start_ref[i + 1], start_ref[i])
        count = jnp.where(second, length_ref[i + 1], length_ref[i])
        bounds += [first, first + count]
    own_bounds = pl.ds(pl.multiple_of(core * rows, rows), rows)
    bound_ref[own_bounds, :] = jnp.concatenate(bounds, axis=0).astype(jnp.float32)

    pl.semaphore_wait(barrier, half + core + quarter)

    def bias_copy(place, target):
        return pltpu.make_async_remote_copy(
            src_ref=bias_ref.at[own],
            dst_ref=bias_ref.at[place],
            send_sem=bias_send,
            recv_sem=bias_recv.at[place],
            device_id={"row": target},
            device_id_type=MESH,
        )

    def mate_copy(ref, slot):
        return pltpu.make_async_remote_copy(
            src_ref=ref.at[own_bounds],
            dst_ref=ref.at[own_bounds],
            send_sem=mate_send.at[slot],
            recv_sem=mate_recv.at[slot],
            device_id={"row": mate},
            device_id_type=MESH,
        )

    def far(step):
        late = step // quarter
        return other(chip, chips - 2 - 2 * (step - quarter * late) + late, chips)

    def send_far(step, carry):
        bias_copy(place_of_me, far(step) * 2 + 1).start()
        return carry

    def send_near(step, carry):
        bias_copy(place_of_me, other(chip, step, chips) * 2).start()
        return carry

    def pass_on(place):
        return pltpu.make_async_remote_copy(
            src_ref=bias_ref.at[place],
            dst_ref=bias_ref.at[place],
            send_sem=pass_send,
            recv_sem=bias_recv.at[place],
            device_id={"row": other(chip, 1, chips) * 2 + 1},
            device_id_type=MESH,
        )

    x_copy, bound_copy = mate_copy(x_ref, 0), mate_copy(bound_ref, 1)
    lax.fori_loop(0, quarter, send_far, 0, unroll=unrolled)
    x_copy.start()
    bound_copy.start()
    lax.fori_loop(1, half, send_near, 0, unroll=unrolled)

    @pl.when(core == 1)
    def _():
        bias_copy(place_of_me, mate).start()

    for copy in weights_in:
        copy.wait()
    lane = lax.broadcasted_iota(jnp.int32, (1, channels), 1) // head
    masks = [(lane == h).astype(jnp.float32).astype(jnp.bfloat16) for h in range(H)]
    factor = LOG2E / head**0.5

    def project(i, couple, side):
        row = x_ref[i]
        asking = x_ref[i, pl.ds(pl.multiple_of(asked_half * (width // 2), width // 2), width // 2), :]
        asked = jnp.dot(asking, asking_ref[...], preferred_element_type=jnp.float32)
        query_ref[i] = asked[:, :channels].astype(jnp.bfloat16)
        gate = asked[:, channels:].astype(jnp.bfloat16).astype(jnp.float32)
        sig_ref[i] = jax.nn.sigmoid(gate)
        given = jnp.dot(row, giving_ref[...], preferred_element_type=jnp.float32)
        given = given.astype(jnp.bfloat16)
        span = slice(side * channels, (side + 1) * channels)
        key_ref[couple, :, span] = given[:, :channels]
        value_ref[couple, :, span] = given[:, channels:]

    spot = lax.broadcasted_iota(jnp.int32, (width, lanes), 0).astype(jnp.float32)
    wide = 2 * rows
    nothing = jnp.zeros((wide, channels), jnp.bfloat16)

    def score(couple):
        first = bound_ref[pl.ds(2 * couple, 1), :]
        last = bound_ref[pl.ds(2 * couple + 1, 1), :]
        valid = (spot >= first) & (spot < last)
        keys = key_ref[couple]
        for at in range(half):
            queries = [query_ref[2 * couple + side, at * wide : (at + 1) * wide, :] for side in range(2)]
            spread_out = [jnp.concatenate([queries[0] * m, nothing], axis=1) for m in masks]
            spread_out += [jnp.concatenate([nothing, queries[1] * m], axis=1) for m in masks]
            part = lax.dot_general(
                keys, jnp.concatenate(spread_out, axis=0), NT, preferred_element_type=jnp.float32
            )
            score_ref[at, couple] = jnp.where(valid, part * factor, jnp.float32(-1e30))

    def prepare(which):
        first = which * (rows // 2)
        if width <= 128:
            for at in range(rows):
                project(which * rows + at, first + at // 2, at % 2)
            for at in range(rows // 2):
                score(first + at)
        else:

            @pl.loop(0, rows // 2)
            def _(at):
                for side in range(2):
                    project(which * rows + 2 * at + side, first + at, side)
                score(first + at)

    @pl.loop(0, 2)
    def _(turn_at):
        @pl.when(turn_at == 1)
        def _():
            x_copy.wait_recv()
            bound_copy.wait_recv()

        prepare(core + turn_at - 2 * core * turn_at)

    def turn(at):
        blocks = []
        for h in range(H):
            blocks += [bias_ref[at * 2, h], bias_ref[at * 2 + 1, h]]
        turned_ref[...] = jnp.concatenate(blocks * 2, axis=0).T

    def attend(place, couple):
        t = score_ref[place, couple] + turned_ref[...]
        raised = jnp.exp2(t - jnp.max(t, axis=0, keepdims=True))
        total = jnp.sum(raised, axis=0, keepdims=True)
        weights = (raised * (1.0 / total)).astype(jnp.bfloat16).T
        columns = pl.ds(pl.multiple_of(place * wide, wide), wide)
        results = []
        for side in range(2):
            mixed = jnp.dot(
                weights[side * (lanes // 2) : (side + 1) * (lanes // 2)],
                value_ref[couple, :, side * channels : (side + 1) * channels],
                preferred_element_type=jnp.float32,
            )
            attended = mixed[:wide]
            for h in range(1, H):
                attended = jnp.where(lane == h, mixed[h * wide : (h + 1) * wide], attended)
            gated = sig_ref[2 * couple + side, columns, :] * attended
            results.append(gated.astype(jnp.bfloat16))
        return results

    def out_copy(target, part):
        return pltpu.make_async_remote_copy(
            src_ref=send_ref.at[lax.rem(target, chips), pl.ds(part * rows, rows)],
            dst_ref=out_ref.at[pl.ds(pl.multiple_of(chip * both + part * rows, rows), rows)],
            send_sem=out_send,
            recv_sem=out_recv,
            device_id={"row": target},
            device_id_type=MESH,
        )

    def finish(peer, part):
        place = lax.rem(peer, half)
        gated = []
        for at in range(rows // 2):
            gated += attend(place, part * (rows // 2) + at)
        update = jnp.dot(
            jnp.concatenate(gated, axis=0), wo_ref[...], preferred_element_type=jnp.float32
        ).reshape(rows, 2, rows, channels)
        slab = pl.ds(pl.multiple_of(part * rows, rows), rows)
        for q in range(2):
            target = peer * 2 + q
            send_ref[place * 2 + q, slab] = update[:, q].astype(jnp.bfloat16)

            @pl.when(target != me)
            def _():
                out_copy(target, part).start()

            @pl.when(target == me)
            def _():
                here = pl.ds(pl.multiple_of(chip * both + part * rows, rows), rows)
                out_ref[here] = send_ref[place * 2 + q, slab]

    def peer_at(step):
        return core * far(step) + (1 - core) * other(chip, half - 1 - step, chips)

    def take(step):
        peer = peer_at(step)
        for q in range(2):
            place = lax.rem(peer, half) * 2 + q

            @pl.when(peer * 2 + q != me)
            def _():
                bias_copy(place, mate).wait_recv()

            @pl.when((core == 1) & (step < quarter))
            def _():
                pass_on(place).start()

    @pl.loop(0, half)
    def _(step):
        take(step)
        peer = peer_at(step)
        turn(lax.rem(peer, half))
        pl.loop(0, 2)(lambda part: finish(peer, part))

    x_copy.wait_send()
    bound_copy.wait_send()
    def bias_rest(count, send_sem):
        return pltpu.make_async_remote_copy(
            src_ref=bias_ref.at[pl.ds(0, count)],
            dst_ref=bias_ref.at[pl.ds(0, count)],
            send_sem=send_sem,
            recv_sem=bias_recv.at[0],
            device_id={"row": mate},
            device_id_type=MESH,
        )

    def out_rest(count):
        return pltpu.make_async_remote_copy(
            src_ref=send_ref.at[pl.ds(0, count)],
            dst_ref=out_ref.at[pl.ds(0, count * both)],
            send_sem=out_send,
            recv_sem=out_recv,
            device_id={"row": mate},
            device_id_type=MESH,
        )

    for count, which in ((chips - 1, 0), (chips, 1)):

        @pl.when(core == which)
        def _():
            bias_rest(quarter + half - 1 + which, bias_send).wait_send()
            out_rest(count).wait_send()
            out_rest(count).wait_recv()

    @pl.when(core == 1)
    def _():
        bias_rest(half, pass_send).wait_send()


def local(
    n, pair_map, norm_gain, w_query, w_key, w_value, w_gate, w_bias, w_output, window_start, key_length
):
    rows, width, channels = pair_map.shape
    chips = n // 2
    lanes = H * 4 * rows
    outside = pl.BlockSpec(memory_space=pltpu.HBM)
    return pl.pallas_call(
        functools.partial(kernel, n),
        out_shape=pltpu.VMEM((n * rows, width // n, channels), jnp.bfloat16),
        in_specs=[outside] * 10,
        out_specs=pl.BlockSpec(memory_space=pltpu.VMEM),
        scratch_shapes=[
            pltpu.VMEM((2 * rows, width, channels), jnp.bfloat16),
            pltpu.VMEM((1, channels), jnp.float32),
            pltpu.VMEM((channels, 2 * channels), jnp.bfloat16),
            pltpu.VMEM((channels, 2 * channels), jnp.bfloat16),
            pltpu.VMEM((H, channels), jnp.bfloat16),
            pltpu.VMEM((channels, channels), jnp.bfloat16),
            pltpu.VMEM((chips + 1, H, rows, width), jnp.float32),
            pltpu.VMEM((width, lanes), jnp.float32),
            pltpu.VMEM((chips // 2, rows, width, lanes), jnp.float32),
            pltpu.VMEM((2 * rows, width // 2, channels), jnp.bfloat16),
            pltpu.VMEM((rows, width, 2 * channels), jnp.bfloat16),
            pltpu.VMEM((rows, width, 2 * channels), jnp.bfloat16),
            pltpu.VMEM((2 * rows, width // 2, channels), jnp.float32),
            pltpu.VMEM((chips, 2 * rows, width // n, channels), jnp.bfloat16),
            pltpu.VMEM((2 * rows, lanes), jnp.float32),
            pltpu.SMEM((rows,), jnp.int32),
            pltpu.SMEM((rows,), jnp.int32),
            pltpu.SemaphoreType.DMA((9 + PIECES,)),
            pltpu.SemaphoreType.DMA,
            pltpu.SemaphoreType.DMA((chips,)),
            pltpu.SemaphoreType.DMA,
            pltpu.SemaphoreType.DMA((2,)),
            pltpu.SemaphoreType.DMA((2,)),
            pltpu.SemaphoreType.DMA,
            pltpu.SemaphoreType.DMA,
        ],
        compiler_params=pltpu.CompilerParams(
            collective_id=0, has_side_effects=True, vmem_limit_bytes=60 * 1024 * 1024
        ),
        name="attend",
    )(
        pair_map,
        norm_gain.reshape(1, channels),
        w_query,
        w_key,
        w_value,
        w_gate,
        w_bias.T,
        w_output,
        window_start,
        key_length,
    )


def solution(mesh):
    return jax.shard_map(
        functools.partial(local, mesh.shape["row"]),
        mesh=mesh,
        in_specs=(
            P(("grp", "row"), None, None),
            P(),
            P(),
            P(),
            P(),
            P(),
            P(),
            P(),
            P(("grp", "row")),
            P(("grp", "row")),
        ),
        out_specs=P("grp", "row", None),
        check_vma=False,
    )
```

```python
import functools
import math

import jax
import jax.numpy as jnp
from jax import lax
from jax.experimental import pallas as pl
from jax.experimental.pallas import tpu as pltpu
from jax.sharding import PartitionSpec as P

H = 4
LOG2E = math.log2(math.e)
MESH = pl.DeviceIdType.MESH
NT = (((1,), (1,)), ((), ()))
TN = (((0,), (0,)), ((), ()))
PIECES = 1


def other(index, step, count):
    result, bit = 0, 1
    while bit < count:
        a, b = index // bit % 2, step // bit % 2
        result = result + (a + b - 2 * a * b) * bit
        bit *= 2
    return result


def kernel(
    n,
    x_hbm,
    gain_hbm,
    wq_hbm,
    wk_hbm,
    wv_hbm,
    wg_hbm,
    wb_hbm,
    wo_hbm,
    start_hbm,
    length_hbm,
    out_ref,
    x_ref,
    gain_ref,
    asking_ref,
    giving_ref,
    wb_ref,
    wo_ref,
    bias_ref,
    turned_ref,
    score_ref,
    query_ref,
    key_ref,
    value_ref,
    sig_ref,
    send_ref,
    bound_ref,
    start_ref,
    length_ref,
    in_sem,
    bias_send,
    bias_recv,
    pass_send,
    mate_send,
    mate_recv,
    out_send,
    out_recv,
):
    both, width, channels = x_ref.shape
    rows = both // 2
    head = channels // H
    chips = n // 2
    half = chips // 2
    lanes = H * 4 * rows
    unrolled = chips <= 8
    me = lax.axis_index("row")
    core, chip = me % 2, me // 2
    mate = me + 1 - 2 * core
    place_of_me = lax.rem(me, chips)
    own = core * chips + (1 - core) * place_of_me
    quarter = half // 2
    side = chip // half
    asked_half = side + core - 2 * side * core
    piece = max(1, rows // PIECES)

    def load(source, target, slot):
        copy = pltpu.make_async_copy(source, target, in_sem.at[slot])
        copy.start()
        return copy

    x_in = [
        load(x_hbm.at[pl.ds(at, piece)], x_ref.at[pl.ds(core * rows + at, piece)], 9 + at)
        for at in range(0, rows, piece)
    ]
    first_in = [load(gain_hbm, gain_ref, 0), load(wb_hbm, wb_ref, 1)]
    barrier = pltpu.get_barrier_semaphore()

    def hello(target):
        pl.semaphore_signal(barrier, inc=1, device_id={"row": target}, device_id_type=MESH)

    def greet_both(peer, when):
        @pl.when(when)
        def _():
            hello(peer * 2)
            hello(peer * 2 + 1)

    def greet_far(at, carry):
        peer = other(chip, chips - 2 - 2 * at, chips)
        greet_both(peer, core == 1)
        return carry

    def greet_near(step, carry):
        peer = other(chip, step, chips)
        greet_both(peer, core == 0)
        return carry

    lax.fori_loop(0, quarter, greet_far, 0, unroll=unrolled)
    lax.fori_loop(1, half, greet_near, 0, unroll=unrolled)

    @pl.when(core == 1)
    def _():
        hello(other(chip, 1, chips) * 2 + 1)

    hello(mate)

    left, right = pl.ds(0, channels), pl.ds(channels, channels)
    window_in = [load(start_hbm, start_ref, 2), load(length_hbm, length_ref, 3)]
    weights_in = [
        load(source, target, 4 + at)
        for at, (source, target) in enumerate(
            (
                (wq_hbm, asking_ref.at[:, left]),
                (wg_hbm, asking_ref.at[:, right]),
                (wk_hbm, giving_ref.at[:, left]),
                (wv_hbm, giving_ref.at[:, right]),
                (wo_hbm, wo_ref),
            )
        )
    ]

    for copy in first_in:
        copy.wait()
    bias_weight = wb_ref[...]
    gain = gain_ref[...]
    ones = jnp.ones((channels, channels), jnp.bfloat16)
    for i in range(rows):
        if i % piece == 0:
            x_in[i // piece].wait()
        row = x_ref[core * rows + i]
        center = jnp.dot(row, ones, preferred_element_type=jnp.float32) * (1.0 / channels)
        values = row.astype(jnp.float32) - center
        spread = jnp.mean(values * values, axis=-1, keepdims=True)
        row = (values * lax.rsqrt(spread + 1e-05) * gain).astype(jnp.bfloat16)
        x_ref[core * rows + i] = row
        local = lax.dot_general(bias_weight, row, NT, preferred_element_type=jnp.float32)
        local = local * LOG2E
        for h in range(H):
            bias_ref[own, h, i : i + 1, :] = local[h : h + 1]
    for copy in window_in:
        copy.wait()
    second = lax.broadcasted_iota(jnp.int32, (1, lanes), 1) // (lanes // 2) == 1
    bounds = []
    for i in range(0, rows, 2):
        first = jnp.where(second, start_ref[i + 1], start_ref[i])
        count = jnp.where(second, length_ref[i + 1], length_ref[i])
        bounds += [first, first + count]
    own_bounds = pl.ds(pl.multiple_of(core * rows, rows), rows)
    bound_ref[own_bounds, :] = jnp.concatenate(bounds, axis=0).astype(jnp.float32)

    pl.semaphore_wait(barrier, half + core + quarter)

    def bias_copy(place, target):
        return pltpu.make_async_remote_copy(
            src_ref=bias_ref.at[own],
            dst_ref=bias_ref.at[place],
            send_sem=bias_send,
            recv_sem=bias_recv.at[place],
            device_id={"row": target},
            device_id_type=MESH,
        )

    def mate_copy(ref, slot):
        return pltpu.make_async_remote_copy(
            src_ref=ref.at[own_bounds],
            dst_ref=ref.at[own_bounds],
            send_sem=mate_send.at[slot],
            recv_sem=mate_recv.at[slot],
            device_id={"row": mate},
            device_id_type=MESH,
        )

    def far(step):
        late = step // quarter
        return other(chip, chips - 2 - 2 * (step - quarter * late) + late, chips)

    def send_far(step, carry):
        bias_copy(place_of_me, far(step) * 2 + 1).start()
        return carry

    def send_near(step, carry):
        bias_copy(place_of_me, other(chip, step, chips) * 2).start()
        return carry

    def pass_on(place):
        return pltpu.make_async_remote_copy(
            src_ref=bias_ref.at[place],
            dst_ref=bias_ref.at[place],
            send_sem=pass_send,
            recv_sem=bias_recv.at[place],
            device_id={"row": other(chip, 1, chips) * 2 + 1},
            device_id_type=MESH,
        )

    x_copy, bound_copy = mate_copy(x_ref, 0), mate_copy(bound_ref, 1)
    lax.fori_loop(0, quarter, send_far, 0, unroll=unrolled)
    x_copy.start()
    bound_copy.start()
    lax.fori_loop(1, half, send_near, 0, unroll=unrolled)

    @pl.when(core == 1)
    def _():
        bias_copy(place_of_me, mate).start()

    for copy in weights_in:
        copy.wait()
    lane = lax.broadcasted_iota(jnp.int32, (1, channels), 1) // head
    masks = [(lane == h).astype(jnp.float32).astype(jnp.bfloat16) for h in range(H)]
    factor = LOG2E / head**0.5

    def project(i, couple, side):
        row = x_ref[i]
        asking = x_ref[i, pl.ds(pl.multiple_of(asked_half * (width // 2), width // 2), width // 2), :]
        asked = jnp.dot(asking, asking_ref[...], preferred_element_type=jnp.float32)
        query_ref[i] = asked[:, :channels].astype(jnp.bfloat16)
        gate = asked[:, channels:].astype(jnp.bfloat16).astype(jnp.float32)
        sig_ref[i] = jax.nn.sigmoid(gate)
        given = jnp.dot(row, giving_ref[...], preferred_element_type=jnp.float32)
        given = given.astype(jnp.bfloat16)
        span = slice(side * channels, (side + 1) * channels)
        key_ref[couple, :, span] = given[:, :channels]
        value_ref[couple, :, span] = given[:, channels:]

    spot = lax.broadcasted_iota(jnp.int32, (width, lanes), 0).astype(jnp.float32)
    wide = 2 * rows
    nothing = jnp.zeros((wide, channels), jnp.bfloat16)

    def score(couple):
        first = bound_ref[pl.ds(2 * couple, 1), :]
        last = bound_ref[pl.ds(2 * couple + 1, 1), :]
        valid = (spot >= first) & (spot < last)
        keys = key_ref[couple]
        for at in range(half):
            queries = [query_ref[2 * couple + side, at * wide : (at + 1) * wide, :] for side in range(2)]
            spread_out = [jnp.concatenate([queries[0] * m, nothing], axis=1) for m in masks]
            spread_out += [jnp.concatenate([nothing, queries[1] * m], axis=1) for m in masks]
            part = lax.dot_general(
                keys, jnp.concatenate(spread_out, axis=0), NT, preferred_element_type=jnp.float32
            )
            score_ref[at, couple] = jnp.where(valid, part * factor, jnp.float32(-1e30))

    def prepare(which):
        first = which * (rows // 2)
        if width <= 128:
            for at in range(rows):
                project(which * rows + at, first + at // 2, at % 2)
            for at in range(rows // 2):
                score(first + at)
        else:

            @pl.loop(0, rows // 2)
            def _(at):
                for side in range(2):
                    project(which * rows + 2 * at + side, first + at, side)
                score(first + at)

    @pl.loop(0, 2)
    def _(turn_at):
        @pl.when(turn_at == 1)
        def _():
            x_copy.wait_recv()
            bound_copy.wait_recv()

        prepare(core + turn_at - 2 * core * turn_at)

    def turn(at):
        blocks = []
        for h in range(H):
            blocks += [bias_ref[at * 2, h], bias_ref[at * 2 + 1, h]]
        turned_ref[...] = jnp.concatenate(blocks * 2, axis=0).T

    def attend(place, couple):
        t = score_ref[place, couple] + turned_ref[...]
        raised = jnp.exp2(t - jnp.max(t, axis=0, keepdims=True))
        total = jnp.sum(raised, axis=0, keepdims=True)
        weights = (raised * (1.0 / total)).astype(jnp.bfloat16).T
        columns = pl.ds(pl.multiple_of(place * wide, wide), wide)
        results = []
        for side in range(2):
            mixed = jnp.dot(
                weights[side * (lanes // 2) : (side + 1) * (lanes // 2)],
                value_ref[couple, :, side * channels : (side + 1) * channels],
                preferred_element_type=jnp.float32,
            )
            attended = mixed[:wide]
            for h in range(1, H):
                attended = jnp.where(lane == h, mixed[h * wide : (h + 1) * wide], attended)
            gated = sig_ref[2 * couple + side, columns, :] * attended
            results.append(gated.astype(jnp.bfloat16))
        return results

    def out_copy(target, part):
        return pltpu.make_async_remote_copy(
            src_ref=send_ref.at[lax.rem(target, chips), pl.ds(part * rows, rows)],
            dst_ref=out_ref.at[pl.ds(pl.multiple_of(chip * both + part * rows, rows), rows)],
            send_sem=out_send,
            recv_sem=out_recv,
            device_id={"row": target},
            device_id_type=MESH,
        )

    def finish(peer, part):
        place = lax.rem(peer, half)
        gated = []
        for at in range(rows // 2):
            gated += attend(place, part * (rows // 2) + at)
        update = jnp.dot(
            jnp.concatenate(gated, axis=0), wo_ref[...], preferred_element_type=jnp.float32
        ).reshape(rows, 2, rows, channels)
        slab = pl.ds(pl.multiple_of(part * rows, rows), rows)
        for q in range(2):
            target = peer * 2 + q
            send_ref[place * 2 + q, slab] = update[:, q].astype(jnp.bfloat16)

            @pl.when(target != me)
            def _():
                out_copy(target, part).start()

            @pl.when(target == me)
            def _():
                here = pl.ds(pl.multiple_of(chip * both + part * rows, rows), rows)
                out_ref[here] = send_ref[place * 2 + q, slab]

    def peer_at(step):
        return core * far(step) + (1 - core) * other(chip, half - 1 - step, chips)

    def take(step):
        peer = peer_at(step)
        for q in range(2):
            place = lax.rem(peer, half) * 2 + q

            @pl.when(peer * 2 + q != me)
            def _():
                bias_copy(place, mate).wait_recv()

    @pl.loop(0, half)
    def _(step):
        take(step)
        peer = peer_at(step)
        turn(lax.rem(peer, half))

        @pl.loop(0, 2)
        def _(part):
            finish(peer, part)

            @pl.when((core == 1) & (step < quarter) & (part == 0))
            def _():
                for q in range(2):
                    pass_on(lax.rem(peer, half) * 2 + q).start()

    x_copy.wait_send()
    bound_copy.wait_send()
    def bias_rest(count, send_sem):
        return pltpu.make_async_remote_copy(
            src_ref=bias_ref.at[pl.ds(0, count)],
            dst_ref=bias_ref.at[pl.ds(0, count)],
            send_sem=send_sem,
            recv_sem=bias_recv.at[0],
            device_id={"row": mate},
            device_id_type=MESH,
        )

    def out_rest(count):
        return pltpu.make_async_remote_copy(
            src_ref=send_ref.at[pl.ds(0, count)],
            dst_ref=out_ref.at[pl.ds(0, count * both)],
            send_sem=out_send,
            recv_sem=out_recv,
            device_id={"row": mate},
            device_id_type=MESH,
        )

    for count, which in ((chips - 1, 0), (chips, 1)):

        @pl.when(core == which)
        def _():
            bias_rest(quarter + half - 1 + which, bias_send).wait_send()
            out_rest(count).wait_send()
            out_rest(count).wait_recv()

    @pl.when(core == 1)
    def _():
        bias_rest(half, pass_send).wait_send()


def local(
    n, pair_map, norm_gain, w_query, w_key, w_value, w_gate, w_bias, w_output, window_start, key_length
):
    rows, width, channels = pair_map.shape
    chips = n // 2
    lanes = H * 4 * rows
    outside = pl.BlockSpec(memory_space=pltpu.HBM)
    return pl.pallas_call(
        functools.partial(kernel, n),
        out_shape=pltpu.VMEM((n * rows, width // n, channels), jnp.bfloat16),
        in_specs=[outside] * 10,
        out_specs=pl.BlockSpec(memory_space=pltpu.VMEM),
        scratch_shapes=[
            pltpu.VMEM((2 * rows, width, channels), jnp.bfloat16),
            pltpu.VMEM((1, channels), jnp.float32),
            pltpu.VMEM((channels, 2 * channels), jnp.bfloat16),
            pltpu.VMEM((channels, 2 * channels), jnp.bfloat16),
            pltpu.VMEM((H, channels), jnp.bfloat16),
            pltpu.VMEM((channels, channels), jnp.bfloat16),
            pltpu.VMEM((chips + 1, H, rows, width), jnp.float32),
            pltpu.VMEM((width, lanes), jnp.float32),
            pltpu.VMEM((chips // 2, rows, width, lanes), jnp.float32),
            pltpu.VMEM((2 * rows, width // 2, channels), jnp.bfloat16),
            pltpu.VMEM((rows, width, 2 * channels), jnp.bfloat16),
            pltpu.VMEM((rows, width, 2 * channels), jnp.bfloat16),
            pltpu.VMEM((2 * rows, width // 2, channels), jnp.float32),
            pltpu.VMEM((chips, 2 * rows, width // n, channels), jnp.bfloat16),
            pltpu.VMEM((2 * rows, lanes), jnp.float32),
            pltpu.SMEM((rows,), jnp.int32),
            pltpu.SMEM((rows,), jnp.int32),
            pltpu.SemaphoreType.DMA((9 + rows,)),
            pltpu.SemaphoreType.DMA,
            pltpu.SemaphoreType.DMA((chips,)),
            pltpu.SemaphoreType.DMA,
            pltpu.SemaphoreType.DMA((2,)),
            pltpu.SemaphoreType.DMA((2,)),
            pltpu.SemaphoreType.DMA,
            pltpu.SemaphoreType.DMA,
        ],
        compiler_params=pltpu.CompilerParams(
            collective_id=0, has_side_effects=True, vmem_limit_bytes=60 * 1024 * 1024
        ),
        name="attend",
    )(
        pair_map,
        norm_gain.reshape(1, channels),
        w_query,
        w_key,
        w_value,
        w_gate,
        w_bias.T,
        w_output,
        window_start,
        key_length,
    )


def solution(mesh):
    return jax.shard_map(
        functools.partial(local, mesh.shape["row"]),
        mesh=mesh,
        in_specs=(
            P(("grp", "row"), None, None),
            P(),
            P(),
            P(),
            P(),
            P(),
            P(),
            P(),
            P(("grp", "row")),
            P(("grp", "row")),
        ),
        out_specs=P("grp", "row", None),
        check_vma=False,
    )
```
